256 devices in a mesh: pert: 8 (over z), gene: 32 (over x, y, core).
Axes of the slice: x: 4, y: 4, z: 8, core: 2. Of those that a mesh axis runs over, the one named last changes fastest.
Arguments:
- tensor: bfloat16 [8192, 8, 16384], P('pert', None, 'gene'), may hold values from -2400 to 2400
- pert_factor: bfloat16 [8192, 128], P('pert'), may hold values from -10 to 10
- context_factor: bfloat16 [8, 128], replicated, may hold values from -3 to 3
Outputs:
- gene_factor: bfloat16 [16384, 128], P('gene')
- pert_updated: bfloat16 [8192, 128], P('pert')
The draws below stay inside these ranges and needn't reach their ends.
All inputs are finite; a program needn't handle non-finite values.
Results may differ from the reference program's by a relative error of at most 0.0042.
Values may be sent and summed in bfloat16 or wider, within the bound.
No kernel may reach another device: no remote copies, remote signals or barrier semaphores. Data moves between devices by JAX's collectives and lax.ppermute only.
A program may use at most 64 MiB of HBM per device.

```python
import math
import jax
import jax.numpy as jnp
from jax import lax

R = 128
K = 8
I_DEV = 1024
J_DEV = 512
PERTS = 8192
GENES = 16384
N_PERT = 8
N_GENE = 32


def draw_pert_factor(key, part):
    key_scale, key_base = jax.random.split(key, 2)
    scales = jnp.exp(jax.random.uniform(key_scale, (PERTS, 1), jnp.float32, math.log(0.3), math.log(3.0)))
    values = jax.random.normal(key_base, (PERTS, R), jnp.float32) * scales
    return jnp.clip(values, -10.0, 10.0).astype(jnp.bfloat16)


def draw_tensor(key, part):
    key_rough, key_values = jax.random.split(jax.random.fold_in(key, 17), 2)
    place = jnp.arange(GENES, dtype=jnp.float32) / GENES
    rough = jnp.exp(jax.random.uniform(key_rough, (GENES,), jnp.float32, 0.0, math.log(4.0)))
    column_scale = 32.0 * jnp.exp(math.log(3.0) * place) * rough
    values = jnp.clip(jax.random.normal(key_values, (PERTS, K, GENES), jnp.float32), -6.0, 6.0)
    return (values * column_scale[None, None, :]).astype(jnp.bfloat16)


def gaussian(stream_key, dims, scale, bound, held_as=jnp.bfloat16):
    return jnp.clip(scale * jax.random.normal(stream_key, dims, jnp.float32), -bound, bound).astype(held_as)


def setup_inputs(seed: int = 0) -> dict:
    streams_of = jax.random.split(jax.random.key(seed), 4)
    tensor = draw_tensor(jax.random.fold_in(streams_of[3], 71), 0)
    pert_factor = draw_pert_factor(jax.random.fold_in(streams_of[3], 71), 0)
    context_factor = gaussian(streams_of[2], (K, R), 0.6, 3.0)
    return {"tensor": tensor, "pert_factor": pert_factor, "context_factor": context_factor}


epsilon = 1e-06

def solve_gram(rhs, gram):
    lower = jnp.linalg.cholesky(gram)
    half = lax.linalg.triangular_solve(lower, rhs, left_side=False, lower=True, transpose_a=True)
    return lax.linalg.triangular_solve(lower, half, left_side=False, lower=True, transpose_a=False)

def reference(tensor, pert_factor, context_factor):
    context32 = context_factor.astype(jnp.float32)
    gram_b = jnp.dot(context_factor.T.astype(jnp.float32), context_factor.astype(jnp.float32), preferred_element_type=jnp.float32)
    gram_a = jnp.dot(pert_factor.T.astype(jnp.float32), pert_factor.astype(jnp.float32), preferred_element_type=jnp.float32)
    tensor_blocks = tensor.reshape(N_PERT, I_DEV, K, J_DEV * N_GENE)
    factor_blocks = pert_factor.reshape(N_PERT, I_DEV, R)

    def gene_step(summed, blocks_pair):
        tensor_block, factor_block = blocks_pair
        partial_sum = jnp.einsum('ikj,ir->kjr', tensor_block.astype(jnp.float32), factor_block.astype(jnp.float32))
        return (summed + partial_sum, None)
    summed, unused = lax.scan(gene_step, jnp.zeros((K, J_DEV * N_GENE, R), jnp.float32), (tensor_blocks, factor_blocks))
    mttkrp_c = lax.optimization_barrier(jnp.sum(summed * context32[:, None, :], axis=0))
    solved_c = solve_gram(mttkrp_c, gram_a * gram_b)
    gram_s = jnp.dot(solved_c.T.astype(jnp.float32), solved_c.astype(jnp.float32), precision=lax.Precision.HIGHEST, preferred_element_type=jnp.float32)
    scale_c = jnp.sqrt(jnp.diagonal(gram_s) / (J_DEV * N_GENE) + epsilon)
    gene_factor = (solved_c / scale_c[None, :]).astype(jnp.bfloat16)
    gram_c = gram_s / (scale_c[:, None] * scale_c[None, :])
    gene32 = gene_factor.astype(jnp.float32)

    def pert_block(tensor_block):
        partial_sum = jnp.einsum('ikj,jr->ikr', tensor_block.astype(jnp.float32), gene32)
        return lax.optimization_barrier(jnp.sum(partial_sum * context32[None, :, :], axis=1))
    mttkrp_a = lax.map(pert_block, tensor_blocks).reshape(N_PERT * I_DEV, R)
    solved_a = solve_gram(mttkrp_a, gram_c * gram_b)
    scale_a = jnp.sqrt(lax.optimization_barrier(jnp.mean(solved_a * solved_a, axis=0)) + epsilon)
    pert_updated = (solved_a / scale_a[None, :]).astype(jnp.bfloat16)
    return (gene_factor, pert_updated)
```

```python
import functools

import jax
import jax.numpy as jnp
from jax import lax
from jax.experimental import pallas as pl
from jax.experimental.pallas import tpu as pltpu
from jax.sharding import PartitionSpec as P

epsilon = 1e-06
f32 = jnp.float32
bf16 = jnp.bfloat16
HIGHEST = lax.Precision.HIGHEST


def dot(a, b, dims=((1,), (0,)), precision=None):
    return lax.dot_general(a, b, (dims, ((), ())), precision=precision, preferred_element_type=f32)


def split(x):
    hi = x.astype(bf16)
    return hi, (x - hi.astype(f32)).astype(bf16)


def dot_split(a, b):
    n = b.shape[1]
    right = jnp.concatenate(split(b), axis=1)
    product = dot(jnp.concatenate(split(a), axis=1), jnp.concatenate([right, right], axis=0))
    return product[:, :n] + product[:, n:]


def eye(n):
    return (
        lax.broadcasted_iota(jnp.int32, (n, n), 0) == lax.broadcasted_iota(jnp.int32, (n, n), 1)
    ).astype(f32)


def diagonal(a, unit):
    picked = a * unit
    return jnp.sum(picked, axis=0, keepdims=True), jnp.sum(picked, axis=1, keepdims=True)


def row_norm(a):
    return jnp.max(jnp.sum(jnp.abs(a), axis=1, keepdims=True))


def inverse(a):
    unit = eye(a.shape[0])
    diag_row, diag_col = diagonal(a, unit)
    scale_row, scale_col = lax.rsqrt(diag_row), lax.rsqrt(diag_col)
    scaled = a * scale_col * scale_row
    off = row_norm(unit - scaled)
    far = off >= 0.95
    alpha = jnp.where(far, 1.0 / (1.0 + off), 1.0)
    r = unit - alpha * scaled
    x = alpha * (unit + r)
    r = dot_split(r, r)
    n = a.shape[0]

    def advance(x, r):
        product = dot_split(jnp.concatenate([x, r], axis=0), r)
        return x + product[:n, :], product[n:, :]

    def measured(state):
        x, r, _, count = state
        x, r = advance(x, r)
        return x, r, row_norm(r), count + 1

    def bounded(state):
        x, r, bound = state
        return *advance(x, r), bound * bound

    x, r, bound, _ = lax.while_loop(
        lambda s: jnp.logical_and(s[2] > 0.5, s[3] < 40), measured, (x, r, row_norm(r), 0)
    )
    x, r, bound = lax.while_loop(lambda s: s[2] > 1e-7, bounded, (x, r, jnp.minimum(bound, 0.5)))

    def newton(_, x):
        return x + dot_split(x, unit - dot(scaled, x, precision=HIGHEST))

    x = lax.fori_loop(0, jnp.where(far, 4, 1), newton, x)
    return x * scale_col * scale_row


def gram_of(context):
    return dot(context, context, ((0,), (0,)))


def gene_products(tensor_ref, factor_ref, context_ref, out_ref, spread, pattern, total, gram):
    step = pl.program_id(0)
    contexts, rank = context_ref.shape
    rows = factor_ref.shape[0]
    wide = rows * contexts

    @pl.when(step == 0)
    def _():
        lane = lax.broadcasted_iota(jnp.int32, (rows, wide), 1)
        row = lax.broadcasted_iota(jnp.int32, (rows, wide), 0)
        spread[...] = (lane // contexts == row).astype(f32).astype(bf16)
        lane = lax.broadcasted_iota(jnp.int32, (contexts, wide), 1)
        row = lax.broadcasted_iota(jnp.int32, (contexts, wide), 0)
        each = (lane % contexts == row).astype(f32).astype(bf16)
        pattern[...] = dot(context_ref[...], each, ((0,), (0,)))
        total[...] = jnp.zeros_like(total)
        gram[...] = jnp.zeros_like(gram)

    factor = factor_ref[...]
    hi, lo = split(dot(factor, spread[...], ((0,), (0,))) * pattern[...])
    total[...] += dot(jnp.concatenate([hi, lo], axis=0), tensor_ref[...])
    gram[...] += gram_of(factor)

    @pl.when(step == pl.num_programs(0) - 1)
    def _():
        chunks, height, _ = out_ref.shape
        part = rank // chunks
        genes = height - part
        summed = (total[:rank, :] + total[rank:, :]).T
        for q in range(chunks):
            out_ref[q, :genes, :] = summed[q * genes : (q + 1) * genes, :]
            out_ref[q, genes:, :] = gram[q * part : (q + 1) * part, :]


def sum_and_copy(in_ref, out_ref):
    total = jnp.sum(in_ref[...], axis=0)
    for q in range(out_ref.shape[0]):
        out_ref[q] = total


def pert_products(blocks, held_ref, context_ref, tensor_ref, out_ref, solved_ref, stage, wide, sems):
    copies = []
    height = stage.shape[0] // blocks
    for b in range(blocks):
        rows = pl.ds(b * height, height)
        copy = pltpu.make_async_copy(tensor_ref.at[rows, :], stage.at[rows, :], sems.at[b])
        copy.start()
        copies.append(copy)
    chunks, tall, rank = held_ref.shape
    contexts = context_ref.shape[0]
    part = rank // chunks
    genes = tall - part
    context = context_ref[...]
    gram_a = jnp.concatenate([held_ref[q, genes:, :] for q in range(chunks)], axis=0)
    mttkrp = jnp.concatenate([held_ref[q, :genes, :] for q in range(chunks)], axis=0)
    inv = inverse(gram_a * gram_of(context))
    solved = dot(mttkrp, inv, precision=HIGHEST)
    solved_ref[...] = solved
    gram_s = dot(solved, solved, ((0,), (0,)), precision=HIGHEST)
    targets, out_tall, _ = out_ref.shape
    gram_part = rank // targets
    perts = stage.shape[0] // contexts // targets
    for q in range(targets):
        rest = out_tall - perts - gram_part
        out_ref[q, perts:, :] = jnp.concatenate(
            [gram_s[q * gram_part : (q + 1) * gram_part, :], jnp.zeros((rest, rank), f32)], axis=0
        )
    weights = jnp.concatenate(split(solved), axis=1)
    context32 = context.astype(f32)
    per_block = height // contexts
    for b in range(blocks):
        copies[b].wait()
        product = dot(stage[pl.ds(b * height, height), :], weights)
        wide[...] = product[:, :rank] + product[:, rank:]
        total = wide[pl.ds(0, per_block, stride=contexts), :] * context32[0:1, :]
        for k in range(1, contexts):
            total += wide[pl.ds(k, per_block, stride=contexts), :] * context32[k : k + 1, :]
        here = per_block // perts
        out_ref[pl.ds(b * here, here), :perts, :] = total.reshape(here, perts, rank)


def pert_solve(gene_count, held_ref, context_ref, solved_ref, gene_ref, out_ref, squares_ref):
    chunks, tall, rank = held_ref.shape
    gram_part = rank // chunks
    perts = out_ref.shape[0] // chunks
    gram_s = jnp.concatenate(
        [held_ref[q, perts : perts + gram_part, :] for q in range(chunks)], axis=0
    )
    diag_row, _ = diagonal(gram_s, eye(rank))
    scale_c = jnp.sqrt(diag_row / gene_count + epsilon)
    gene_ref[...] = (solved_ref[...] / scale_c).astype(bf16)
    inv = inverse(gram_s * gram_of(context_ref[...])) * scale_c
    mttkrp = held_ref[:, :perts, :].reshape(out_ref.shape)
    solved = dot(mttkrp, inv, precision=HIGHEST)
    out_ref[...] = solved
    squares = jnp.sum(solved * solved, axis=0, keepdims=True)
    squares_ref[...] = jnp.broadcast_to(squares[None], squares_ref.shape)


def pert_scale(pert_count, held_ref, solved_ref, out_ref):
    squares = jnp.sum(held_ref[...], axis=0)[:1, :]
    scale_a = jnp.sqrt(squares / pert_count + epsilon)
    out_ref[...] = (solved_ref[...] / scale_a).astype(bf16)


def vmem(n):
    return [pl.BlockSpec(memory_space=pltpu.VMEM)] * n


def shards(tensor, pert_factor, context_factor):
    rows_i, contexts, rows_j = tensor.shape
    rank = pert_factor.shape[1]
    n_pert = lax.axis_size("pert")
    n_gene = lax.axis_size("gene")
    flat = tensor.reshape(rows_i * contexts, rows_j)
    blocks = 8
    part_i = rows_i // blocks
    genes = rows_j // n_pert
    tall = genes + rank // n_pert

    partial = pl.pallas_call(
        gene_products,
        grid=(blocks,),
        in_specs=[
            pl.BlockSpec((part_i * contexts, rows_j), lambda b: (b, 0)),
            pl.BlockSpec((part_i, rank), lambda b: (b, 0)),
            pl.BlockSpec((contexts, rank), lambda b: (0, 0)),
        ],
        out_specs=pl.BlockSpec((n_pert, tall, rank), lambda b: (0, 0, 0)),
        out_shape=jax.ShapeDtypeStruct((n_pert, tall, rank), f32),
        scratch_shapes=[
            pltpu.VMEM((part_i, part_i * contexts), bf16),
            pltpu.VMEM((rank, part_i * contexts), f32),
            pltpu.VMEM((2 * rank, rows_j), f32),
            pltpu.VMEM((rank, rank), f32),
        ],
        name="gene_products",
    )(flat, pert_factor, context_factor)
    partial = lax.all_to_all(partial, "pert", 0, 0)
    summed = pl.pallas_call(
        sum_and_copy,
        in_specs=vmem(1),
        out_specs=pl.BlockSpec(memory_space=pltpu.VMEM),
        out_shape=jax.ShapeDtypeStruct(partial.shape, f32),
        name="pert_sum",
    )(partial)
    gathered = lax.all_to_all(summed, "pert", 0, 0)

    perts = rows_i // n_gene
    out_tall = -(-(perts + rank // n_gene) // 8) * 8
    partial, solved_c = pl.pallas_call(
        functools.partial(pert_products, blocks),
        in_specs=vmem(2) + [pl.BlockSpec(memory_space=pl.ANY)],
        out_specs=tuple(vmem(2)),
        out_shape=(
            jax.ShapeDtypeStruct((n_gene, out_tall, rank), f32),
            jax.ShapeDtypeStruct((rows_j, rank), f32),
        ),
        scratch_shapes=[
            pltpu.VMEM((rows_i * contexts, rows_j), bf16),
            pltpu.VMEM((part_i * contexts, rank), f32),
            pltpu.SemaphoreType.DMA((blocks,)),
        ],
        name="pert_products",
    )(gathered, context_factor, flat)
    partial = lax.all_to_all(partial, "gene", 0, 0)
    summed = pl.pallas_call(
        sum_and_copy,
        in_specs=vmem(1),
        out_specs=pl.BlockSpec(memory_space=pltpu.VMEM),
        out_shape=jax.ShapeDtypeStruct(partial.shape, f32),
        name="gene_sum",
    )(partial)
    gathered = lax.all_to_all(summed, "gene", 0, 0)

    gene_factor, solved_a, squares = pl.pallas_call(
        functools.partial(pert_solve, rows_j * n_gene),
        in_specs=vmem(3),
        out_specs=tuple(vmem(3)),
        out_shape=(
            jax.ShapeDtypeStruct((rows_j, rank), bf16),
            jax.ShapeDtypeStruct((rows_i, rank), f32),
            jax.ShapeDtypeStruct((n_pert, 8, rank), f32),
        ),
        name="pert_solve",
    )(gathered, context_factor, solved_c)
    squares = lax.all_to_all(squares, "pert", 0, 0)
    pert_updated = pl.pallas_call(
        functools.partial(pert_scale, rows_i * n_pert),
        in_specs=vmem(2),
        out_specs=pl.BlockSpec(memory_space=pltpu.VMEM),
        out_shape=jax.ShapeDtypeStruct((rows_i, rank), bf16),
        name="pert_scale",
    )(squares, solved_a)
    return (gene_factor, pert_updated)


def solution(mesh):
    return jax.shard_map(
        shards,
        mesh=mesh,
        in_specs=(P("pert", None, "gene"), P("pert", None), P()),
        out_specs=(P("gene", None), P("pert", None)),
        check_vma=False,
    )
```

```python
import functools

import jax
import jax.numpy as jnp
from jax import lax
from jax.experimental import pallas as pl
from jax.experimental.pallas import tpu as pltpu
from jax.sharding import PartitionSpec as P

epsilon = 1e-06
f32 = jnp.float32
bf16 = jnp.bfloat16
HIGHEST = lax.Precision.HIGHEST


def dot(a, b, dims=((1,), (0,)), precision=None):
    return lax.dot_general(a, b, (dims, ((), ())), precision=precision, preferred_element_type=f32)


def split(x):
    hi = x.astype(bf16)
    return hi, (x - hi.astype(f32)).astype(bf16)


def dot_split(a, b):
    n = b.shape[1]
    right = jnp.concatenate(split(b), axis=1)
    product = dot(jnp.concatenate(split(a), axis=1), jnp.concatenate([right, right], axis=0))
    return product[:, :n] + product[:, n:]


def eye(n):
    return (
        lax.broadcasted_iota(jnp.int32, (n, n), 0) == lax.broadcasted_iota(jnp.int32, (n, n), 1)
    ).astype(f32)


def diagonal(a, unit):
    picked = a * unit
    return jnp.sum(picked, axis=0, keepdims=True), jnp.sum(picked, axis=1, keepdims=True)


def row_norm(a):
    return jnp.max(jnp.sum(jnp.abs(a), axis=1, keepdims=True))


def inverse(a):
    unit = eye(a.shape[0])
    diag_row, diag_col = diagonal(a, unit)
    scale_row, scale_col = lax.rsqrt(diag_row), lax.rsqrt(diag_col)
    scaled = a * scale_col * scale_row
    off = row_norm(unit - scaled)
    far = off >= 0.95
    alpha = jnp.where(far, 1.0 / (1.0 + off), 1.0)
    r = unit - alpha * scaled
    x = alpha * (unit + r)
    r = dot_split(r, r)
    n = a.shape[0]

    def advance(x, r):
        product = dot_split(jnp.concatenate([x, r], axis=0), r)
        return x + product[:n, :], product[n:, :]

    def measured(state):
        x, r, _, count = state
        x, r = advance(x, r)
        return x, r, row_norm(r), count + 1

    def bounded(state):
        x, r, bound = state
        return *advance(x, r), bound * bound

    x, r, bound, _ = lax.while_loop(
        lambda s: jnp.logical_and(s[2] > 0.5, s[3] < 40), measured, (x, r, row_norm(r), 0)
    )
    x, r, bound = lax.while_loop(lambda s: s[2] > 1e-7, bounded, (x, r, jnp.minimum(bound, 0.5)))

    def newton(_, x):
        return x + dot_split(x, unit - dot(scaled, x, precision=HIGHEST))

    x = lax.fori_loop(0, jnp.where(far, 4, 1), newton, x)
    return x * scale_col * scale_row


def gram_of(context):
    return dot(context, context, ((0,), (0,)))


def gene_products(blocks, depth, tensor_ref, factor_hbm, context_hbm, out_ref, keep, factor_ref, context_ref, sems, small):
    height = keep.shape[0] // blocks
    copies = []
    for b in range(blocks):
        rows = pl.ds(b * height, height)
        copies.append(pltpu.make_async_copy(tensor_ref.at[rows, :], keep.at[rows, :], sems.at[b]))
    first = pltpu.make_async_copy(factor_hbm, factor_ref, small.at[0])
    second = pltpu.make_async_copy(context_hbm, context_ref, small.at[1])
    first.start()
    second.start()
    for copy in copies[:depth]:
        copy.start()
    contexts, rank = context_ref.shape
    chunks, tall, _ = out_ref.shape
    part = rank // chunks
    genes = tall - part
    first.wait()
    second.wait()
    gram = gram_of(factor_ref[...])
    for q in range(chunks):
        out_ref[q, genes:, :] = gram[q * part : (q + 1) * part, :]
    context32 = context_ref[...].astype(f32)
    perts = height // contexts
    total = jnp.zeros((2 * rank, keep.shape[1]), f32)
    for b in range(blocks):
        factor = factor_ref[pl.ds(b * perts, perts), :].astype(f32)
        rows = (factor[:, None, :] * context32[None]).reshape(height, rank)
        rows = jnp.concatenate(split(rows), axis=1)
        copies[b].wait()
        if b + depth < blocks:
            copies[b + depth].start()
        total += dot(rows, keep[pl.ds(b * height, height), :], ((0,), (0,)))
    summed = (total[:rank, :] + total[rank:, :]).T
    for q in range(chunks):
        out_ref[q, :genes, :] = summed[q * genes : (q + 1) * genes, :]


def sum_and_copy(in_ref, out_ref):
    total = jnp.sum(in_ref[...], axis=0)
    for q in range(out_ref.shape[0]):
        out_ref[q] = total


def add(a_ref, b_ref, out_ref):
    out_ref[...] = a_ref[...] + b_ref[...]


def half_index():
    return lax.rem(lax.axis_index("gene"), 2)


def pert_products(blocks, held_ref, context_ref, tensor_ref, mine_ref, other_ref, solved_ref, gram):
    chunks, tall, rank = held_ref.shape
    contexts = context_ref.shape[0]
    part = rank // chunks
    genes = tall - part
    context = context_ref[...]
    gram_a = jnp.concatenate([held_ref[q, genes:, :] for q in range(chunks)], axis=0)
    mttkrp = jnp.concatenate([held_ref[q, :genes, :] for q in range(chunks)], axis=0)
    inv = inverse(gram_a * gram_of(context))
    solved = dot(mttkrp, inv, precision=HIGHEST)
    solved_ref[...] = solved
    gram[...] = dot(solved, solved, ((0,), (0,)), precision=HIGHEST)
    weights = jnp.concatenate(split(solved), axis=1)
    context32 = context.astype(f32)
    half = tensor_ref.shape[0] // 2
    height = half // blocks
    per_block = height // contexts
    for core, out_ref in ((1 - half_index(), other_ref), (half_index(), mine_ref)):
        targets, out_tall, _ = out_ref.shape
        gram_part = rank // 2 // targets
        perts = half // contexts // targets
        rest = out_tall - perts - gram_part
        here = gram[pl.ds(pl.multiple_of(core * (rank // 2), rank // 2), rank // 2), :]
        for q in range(targets):
            out_ref[q, perts:, :] = jnp.concatenate(
                [here[q * gram_part : (q + 1) * gram_part, :], jnp.zeros((rest, rank), f32)], axis=0
            )
        for b in range(blocks):
            start = pl.multiple_of(core * half + b * height, height)
            product = dot(tensor_ref[pl.ds(start, height), :], weights)
            wide = (product[:, :rank] + product[:, rank:]).reshape(per_block, contexts, rank)
            total = jnp.sum(wide * context32[None], axis=1)
            n = per_block // perts
            out_ref[pl.ds(b * n, n), :perts, :] = total.reshape(n, perts, rank)


def pert_solve(
    gene_count, mine_ref, other_ref, context_ref, solved_ref, gene_ref, out_ref, squares_ref, gram
):
    chunks, tall, rank = mine_ref.shape
    gram_part = rank // 2 // chunks
    perts = out_ref.shape[0] // 2 // chunks
    mine = half_index()
    for core, held_ref in ((mine, mine_ref), (1 - mine, other_ref)):
        rows = jnp.concatenate(
            [held_ref[q, perts : perts + gram_part, :] for q in range(chunks)], axis=0
        )
        gram[pl.ds(pl.multiple_of(core * (rank // 2), rank // 2), rank // 2), :] = rows
    gram_s = gram[...]
    diag_row, _ = diagonal(gram_s, eye(rank))
    scale_c = jnp.sqrt(diag_row / gene_count + epsilon)
    gene_ref[...] = (solved_ref[...] / scale_c).astype(bf16)
    inv = inverse(gram_s * gram_of(context_ref[...])) * scale_c
    half = out_ref.shape[0] // 2
    squares = jnp.zeros((1, rank), f32)
    for core, held_ref in ((mine, mine_ref), (1 - mine, other_ref)):
        mttkrp = held_ref[:, :perts, :].reshape(half, rank)
        solved = dot(mttkrp, inv, precision=HIGHEST)
        out_ref[pl.ds(pl.multiple_of(core * half, half), half), :] = solved
        squares += jnp.sum(solved * solved, axis=0, keepdims=True)
    squares_ref[...] = jnp.broadcast_to(squares[None], squares_ref.shape)


def pert_scale(pert_count, held_ref, solved_ref, out_ref):
    squares = jnp.sum(held_ref[...], axis=0)[:1, :]
    scale_a = jnp.sqrt(squares / pert_count + epsilon)
    out_ref[...] = (solved_ref[...] / scale_a).astype(bf16)


VMEM = pl.BlockSpec(memory_space=pltpu.VMEM)
FAR = pl.BlockSpec(memory_space=pltpu.HBM)


def near(x):
    return pltpu.with_memory_space_constraint(x, pltpu.VMEM)


def far(x):
    return pltpu.with_memory_space_constraint(x, pltpu.HBM)


def call(body, name, inputs, outputs, in_specs=None, scratch=(), limit=16):
    single = not isinstance(outputs, tuple)
    return pl.pallas_call(
        body,
        in_specs=in_specs or [VMEM] * len(inputs),
        out_specs=VMEM if single else (VMEM,) * len(outputs),
        out_shape=outputs,
        scratch_shapes=list(scratch),
        compiler_params=pltpu.CompilerParams(vmem_limit_bytes=limit << 20),
        name=name,
    )(*inputs)


def summed_copies(x, name):
    return call(sum_and_copy, name, (near(x),), pltpu.VMEM(x.shape, f32))


def shards(tensor, pert_factor, context_factor):
    rows_i, contexts, rows_j = tensor.shape
    rank = pert_factor.shape[1]
    n_pert = lax.axis_size("pert")
    n_gene = lax.axis_size("gene")
    flat = tensor.reshape(rows_i * contexts, rows_j)
    blocks = 8
    tall = rows_j // n_pert + rank // n_pert

    partial, kept = call(
        functools.partial(gene_products, blocks, 3),
        "gene_products",
        (far(flat), far(pert_factor), far(context_factor)),
        (pltpu.VMEM((n_pert, tall, rank), f32), pltpu.VMEM(flat.shape, bf16)),
        in_specs=[FAR] * 3,
        scratch=(
            pltpu.VMEM(pert_factor.shape, bf16),
            pltpu.VMEM(context_factor.shape, bf16),
            pltpu.SemaphoreType.DMA((blocks,)),
            pltpu.SemaphoreType.DMA((2,)),
        ),
    )
    partial = lax.all_to_all(partial, "pert", 0, 0)
    gathered = lax.all_to_all(summed_copies(partial, "pert_sum"), "pert", 0, 0)

    chips = n_gene // 2
    perts = rows_i // n_gene
    out_tall = -(-(perts + rank // n_gene) // 8) * 8
    message = pltpu.VMEM((chips, out_tall, rank), f32)
    mine, other, solved_c = call(
        functools.partial(pert_products, 4),
        "pert_products",
        (near(gathered), context_factor, near(kept)),
        (message, message, pltpu.VMEM((rows_j, rank), f32)),
        scratch=(pltpu.VMEM((rank, rank), f32),),
    )
    swap = [(i, i ^ 1) for i in range(n_gene)]
    groups = [[2 * i + core for i in range(chips)] for core in range(2)]
    other = lax.ppermute(other, "gene", swap)
    partial = call(add, "core_sum", (near(mine), near(other)), message)
    partial = lax.all_to_all(partial, "gene", 0, 0, axis_index_groups=groups)
    mine = lax.all_to_all(
        summed_copies(partial, "gene_sum"), "gene", 0, 0, axis_index_groups=groups
    )
    other = lax.ppermute(mine, "gene", swap)

    gene_factor, solved_a, squares = call(
        functools.partial(pert_solve, rows_j * n_gene),
        "pert_solve",
        (near(mine), near(other), context_factor, near(solved_c)),
        (
            jax.ShapeDtypeStruct((rows_j, rank), bf16),
            pltpu.VMEM((rows_i, rank), f32),
            pltpu.VMEM((n_pert, 8, rank), f32),
        ),
        scratch=(pltpu.VMEM((rank, rank), f32),),
    )
    squares = lax.all_to_all(squares, "pert", 0, 0)
    pert_updated = call(
        functools.partial(pert_scale, rows_i * n_pert),
        "pert_scale",
        (near(squares), near(solved_a)),
        jax.ShapeDtypeStruct((rows_i, rank), bf16),
    )
    return (gene_factor, pert_updated)


def solution(mesh):
    return jax.shard_map(
        shards,
        mesh=mesh,
        in_specs=(P("pert", None, "gene"), P("pert", None), P()),
        out_specs=(P("gene", None), P("pert", None)),
        check_vma=False,
    )
```

```python
import functools

import jax
import jax.numpy as jnp
from jax import lax
from jax.experimental import pallas as pl
from jax.experimental.pallas import tpu as pltpu
from jax.sharding import PartitionSpec as P

epsilon = 1e-06
f32 = jnp.float32
bf16 = jnp.bfloat16
HIGHEST = lax.Precision.HIGHEST


def dot(a, b, dims=((1,), (0,)), precision=None):
    return lax.dot_general(a, b, (dims, ((), ())), precision=precision, preferred_element_type=f32)


def split(x):
    hi = x.astype(bf16)
    return hi, (x - hi.astype(f32)).astype(bf16)


def dot_split(a, b):
    n = b.shape[1]
    right = jnp.concatenate(split(b), axis=1)
    product = dot(jnp.concatenate(split(a), axis=1), jnp.concatenate([right, right], axis=0))
    return product[:, :n] + product[:, n:]


def eye(n):
    return (
        lax.broadcasted_iota(jnp.int32, (n, n), 0) == lax.broadcasted_iota(jnp.int32, (n, n), 1)
    ).astype(f32)


def diagonal(a, unit):
    picked = a * unit
    return jnp.sum(picked, axis=0, keepdims=True), jnp.sum(picked, axis=1, keepdims=True)


def row_norm(a):
    return jnp.max(jnp.sum(jnp.abs(a), axis=1, keepdims=True))


def inverse(a):
    unit = eye(a.shape[0])
    diag_row, diag_col = diagonal(a, unit)
    scale_row, scale_col = lax.rsqrt(diag_row), lax.rsqrt(diag_col)
    scaled = a * scale_col * scale_row
    off = row_norm(unit - scaled)
    far_off = off >= 0.95
    alpha = jnp.where(far_off, 1.0 / (1.0 + off), 1.0)
    r = unit - alpha * scaled
    x = alpha * (unit + r)
    r = dot_split(r, r)
    n = a.shape[0]

    def advance(x, r):
        product = dot_split(jnp.concatenate([x, r], axis=0), r)
        return x + product[:n, :], product[n:, :]

    def measured(state):
        x, r, _, count = state
        x, r = advance(x, r)
        return x, r, row_norm(r), count + 1

    def bounded(state):
        x, r, bound = state
        return *advance(x, r), bound * bound

    def newton(_, x):
        return x + dot_split(x, unit - dot(scaled, x, precision=HIGHEST))

    x, r, bound, _ = lax.while_loop(
        lambda s: jnp.logical_and(s[2] > 0.95, s[3] < 40),
        measured,
        (x, r, jnp.where(far_off, 1.0, off * off), 0),
    )
    x, r, bound = lax.while_loop(lambda s: s[2] > 1e-7, bounded, (x, r, jnp.minimum(bound, 0.95)))
    x = lax.fori_loop(0, jnp.where(far_off, 4, jnp.where(off > 0.8, 1, 0)), newton, x)
    return x * scale_col * scale_row


def gram_of(context):
    return dot(context, context, ((0,), (0,)))


def gene_products(
    blocks, tensor_ref, factor_hbm, context_hbm, out_ref, keep, factor_ref, context_ref, left, sems, small
):
    height = keep.shape[0] // blocks
    copies = []
    for b in range(blocks):
        rows = pl.ds(b * height, height)
        copies.append(pltpu.make_async_copy(tensor_ref.at[rows, :], keep.at[rows, :], sems.at[b]))
    first = pltpu.make_async_copy(factor_hbm, factor_ref, small.at[0])
    second = pltpu.make_async_copy(context_hbm, context_ref, small.at[1])
    first.start()
    second.start()
    copies[0].start()
    copies[1].start()
    contexts, rank = context_ref.shape
    chunks, tall, _ = out_ref.shape
    part = rank // chunks
    genes = tall - part
    first.wait()
    second.wait()
    gram = gram_of(factor_ref[...])
    for q in range(chunks):
        out_ref[q, genes:, :] = gram[q * part : (q + 1) * part, :]
    context32 = context_ref[...].astype(f32)
    perts = height // contexts

    def build(b):
        factor = factor_ref[pl.ds(b * perts, perts), :].astype(f32)
        rows = (factor[:, None, :] * context32[None]).reshape(height, rank)
        left[b % 2, :rank, :], left[b % 2, rank:, :] = split(rows.T)

    build(0)
    total = None
    for b in range(blocks):
        copies[b].wait()
        if b + 2 < blocks:
            copies[b + 2].start()
        if b + 1 < blocks:
            build(b + 1)
        product = dot(left[b % 2], keep[pl.ds(b * height, height), :])
        total = product if total is None else total + product
    summed = (total[:rank, :] + total[rank:, :]).T
    for q in range(chunks):
        out_ref[q, :genes, :] = summed[q * genes : (q + 1) * genes, :]


def sum_and_copy(in_ref, out_ref):
    total = jnp.sum(in_ref[...], axis=0)
    for q in range(out_ref.shape[0]):
        out_ref[q] = total


def add(a_ref, b_ref, out_ref):
    out_ref[...] = a_ref[...] + b_ref[...]


def half_index():
    return lax.rem(lax.axis_index("gene"), 2)


def contract(blocks, core, tensor_ref, weights, context, gram_ref, out_ref):
    rank = gram_ref.shape[0]
    contexts = context.shape[0]
    context32 = context.astype(f32)
    half = tensor_ref.shape[0] // 2
    height = half // blocks
    per_block = height // contexts
    targets = out_ref.shape[0]
    perts = half // contexts // targets
    out_ref[:, perts:, :] = gram_ref[...].reshape(targets, rank // targets, rank)
    for b in range(blocks):
        start = pl.multiple_of(core * half + b * height, height)
        product = dot(tensor_ref[pl.ds(start, height), :], weights)
        wide = (product[:, :rank] + product[:, rank:]).reshape(per_block, contexts, rank)
        total = jnp.sum(wide * context32[None], axis=1)
        n = per_block // perts
        out_ref[pl.ds(b * n, n), :perts, :] = total.reshape(n, perts, rank)


def gene_solve(blocks, held_ref, context_ref, tensor_ref, other_ref, solved_ref, weights_ref, gram_ref):
    chunks, tall, rank = held_ref.shape
    genes = tall - rank // chunks
    context = context_ref[...]
    gram_a = jnp.concatenate([held_ref[q, genes:, :] for q in range(chunks)], axis=0)
    mttkrp = jnp.concatenate([held_ref[q, :genes, :] for q in range(chunks)], axis=0)
    inv = inverse(gram_a * gram_of(context))
    solved = dot(mttkrp, inv, precision=HIGHEST)
    solved_ref[...] = solved
    weights = jnp.concatenate(split(solved), axis=1)
    weights_ref[...] = weights
    product = dot(weights, weights, ((0,), (0,)))
    product = product[:, :rank] + product[:, rank:]
    gram_ref[...] = product[:rank, :] + product[rank:, :]
    contract(blocks, 1 - half_index(), tensor_ref, weights, context, gram_ref, other_ref)


def pert_products(blocks, weights_ref, context_ref, tensor_ref, gram_ref, mine_ref):
    contract(
        blocks, half_index(), tensor_ref, weights_ref[...], context_ref[...], gram_ref, mine_ref
    )


def pert_inverse(gene_count, mine_ref, context_ref, solved_ref, gene_ref, inv_ref):
    chunks, tall, rank = mine_ref.shape
    perts = tall - rank // chunks
    gram_s = mine_ref[:, perts:, :].reshape(rank, rank)
    diag_row, _ = diagonal(gram_s, eye(rank))
    scale_c = jnp.sqrt(diag_row / gene_count + epsilon)
    gene_ref[...] = (solved_ref[...] / scale_c).astype(bf16)
    inv_ref[...] = inverse(gram_s * gram_of(context_ref[...])) * scale_c


def pert_solve(mine_ref, other_ref, inv_ref, out_ref, squares_ref):
    chunks, tall, rank = mine_ref.shape
    perts = tall - rank // chunks
    inv = inv_ref[...]
    mine = half_index()
    half = out_ref.shape[0] // 2
    squares = []
    for core, held_ref in ((mine, mine_ref), (1 - mine, other_ref)):
        mttkrp = held_ref[:, :perts, :].reshape(half, rank)
        solved = dot(mttkrp, inv, precision=HIGHEST)
        out_ref[pl.ds(pl.multiple_of(core * half, half), half), :] = solved
        squares.append(jnp.sum(solved * solved, axis=0, keepdims=True))
    squares_ref[...] = jnp.broadcast_to((squares[0] + squares[1])[None], squares_ref.shape)


def pert_scale(pert_count, held_ref, solved_ref, out_ref):
    squares = jnp.sum(held_ref[...], axis=0)
    scale_a = jnp.sqrt(squares / pert_count + epsilon)
    out_ref[...] = (solved_ref[...] / scale_a).astype(bf16)


VMEM = pl.BlockSpec(memory_space=pltpu.VMEM)
FAR = pl.BlockSpec(memory_space=pltpu.HBM)


def near(x):
    return pltpu.with_memory_space_constraint(x, pltpu.VMEM)


def far(x):
    return pltpu.with_memory_space_constraint(x, pltpu.HBM)


def call(body, name, inputs, outputs, in_specs=None, scratch=(), limit=16):
    single = not isinstance(outputs, tuple)
    return pl.pallas_call(
        body,
        in_specs=in_specs or [VMEM] * len(inputs),
        out_specs=VMEM if single else (VMEM,) * len(outputs),
        out_shape=outputs,
        scratch_shapes=list(scratch),
        compiler_params=pltpu.CompilerParams(vmem_limit_bytes=limit << 20),
        name=name,
    )(*inputs)


def summed_copies(x, name):
    return call(sum_and_copy, name, (near(x),), pltpu.VMEM(x.shape, f32))


def shards(tensor, pert_factor, context_factor):
    rows_i, contexts, rows_j = tensor.shape
    rank = pert_factor.shape[1]
    n_pert = lax.axis_size("pert")
    n_gene = lax.axis_size("gene")
    flat = tensor.reshape(rows_i * contexts, rows_j)
    blocks = 4
    tall = rows_j // n_pert + rank // n_pert

    partial, kept = call(
        functools.partial(gene_products, blocks),
        "gene_products",
        (far(flat), far(pert_factor), far(context_factor)),
        (pltpu.VMEM((n_pert, tall, rank), f32), pltpu.VMEM(flat.shape, bf16)),
        in_specs=[FAR] * 3,
        scratch=(
            pltpu.VMEM(pert_factor.shape, bf16),
            pltpu.VMEM(context_factor.shape, bf16),
            pltpu.VMEM((2, 2 * rank, flat.shape[0] // blocks), bf16),
            pltpu.SemaphoreType.DMA((blocks,)),
            pltpu.SemaphoreType.DMA((2,)),
        ),
    )
    partial = lax.all_to_all(partial, "pert", 0, 0)
    gathered = lax.all_to_all(summed_copies(partial, "pert_sum"), "pert", 0, 0)

    chips = n_gene // 2
    perts = rows_i // n_gene
    message = pltpu.VMEM((chips, perts + rank // chips, rank), f32)
    square = pltpu.VMEM((rank, rank), f32)
    kept = near(kept)
    other, solved_c, weights, gram_s = call(
        functools.partial(gene_solve, 4),
        "gene_solve",
        (near(gathered), context_factor, kept),
        (
            message,
            pltpu.VMEM((rows_j, rank), f32),
            pltpu.VMEM((rows_j, 2 * rank), bf16),
            square,
        ),
    )
    swap = [(i, i ^ 1) for i in range(n_gene)]
    groups = [[2 * i + core for i in range(chips)] for core in range(2)]
    other = lax.ppermute(other, "gene", swap)
    mine = call(
        functools.partial(pert_products, 4),
        "pert_products",
        (near(weights), context_factor, kept, near(gram_s)),
        message,
    )
    partial = call(add, "core_sum", (near(mine), near(other)), message)
    partial = lax.all_to_all(partial, "gene", 0, 0, axis_index_groups=groups)
    mine = lax.all_to_all(
        summed_copies(partial, "gene_sum"), "gene", 0, 0, axis_index_groups=groups
    )
    other = lax.ppermute(mine, "gene", swap)
    mine = near(mine)
    gene_factor, inv = call(
        functools.partial(pert_inverse, rows_j * n_gene),
        "pert_inverse",
        (mine, context_factor, near(solved_c)),
        (jax.ShapeDtypeStruct((rows_j, rank), bf16), square),
    )
    solved_a, squares = call(
        pert_solve,
        "pert_solve",
        (mine, near(other), near(inv)),
        (pltpu.VMEM((rows_i, rank), f32), pltpu.VMEM((n_pert, 1, rank), f32)),
    )
    squares = lax.all_to_all(squares, "pert", 0, 0)
    pert_updated = call(
        functools.partial(pert_scale, rows_i * n_pert),
        "pert_scale",
        (near(squares), near(solved_a)),
        jax.ShapeDtypeStruct((rows_i, rank), bf16),
    )
    return (gene_factor, pert_updated)


def solution(mesh):
    return jax.shard_map(
        shards,
        mesh=mesh,
        in_specs=(P("pert", None, "gene"), P("pert", None), P()),
        out_specs=(P("gene", None), P("pert", None)),
        check_vma=False,
    )
```

```python
import functools

import jax
import jax.numpy as jnp
from jax import lax
from jax.experimental import pallas as pl
from jax.experimental.pallas import tpu as pltpu
from jax.sharding import PartitionSpec as P

epsilon = 1e-06
f32 = jnp.float32
bf16 = jnp.bfloat16
HIGHEST = lax.Precision.HIGHEST


def dot(a, b, dims=((1,), (0,)), precision=None):
    return lax.dot_general(a, b, (dims, ((), ())), precision=precision, preferred_element_type=f32)


def split(x):
    hi = x.astype(bf16)
    return hi, (x - hi.astype(f32)).astype(bf16)


def dot_split(a, b):
    n = b.shape[1]
    right = jnp.concatenate(split(b), axis=1)
    product = dot(jnp.concatenate(split(a), axis=1), jnp.concatenate([right, right], axis=0))
    return product[:, :n] + product[:, n:]


def eye(n):
    return (
        lax.broadcasted_iota(jnp.int32, (n, n), 0) == lax.broadcasted_iota(jnp.int32, (n, n), 1)
    ).astype(f32)


def diagonal(a, unit):
    picked = a * unit
    return jnp.sum(picked, axis=0, keepdims=True), jnp.sum(picked, axis=1, keepdims=True)


def row_norm(a):
    return jnp.max(jnp.sum(jnp.abs(a), axis=1, keepdims=True))


def inverse(a):
    unit = eye(a.shape[0])
    diag_row, diag_col = diagonal(a, unit)
    scale_row, scale_col = lax.rsqrt(diag_row), lax.rsqrt(diag_col)
    scaled = a * scale_col * scale_row
    off = row_norm(unit - scaled)
    far_off = off >= 0.95
    alpha = jnp.where(far_off, 1.0 / (1.0 + off), 1.0)
    r = unit - alpha * scaled
    x = alpha * (unit + r)
    r = dot_split(r, r)
    n = a.shape[0]

    def advance(x, r):
        product = dot_split(jnp.concatenate([x, r], axis=0), r)
        return x + product[:n, :], product[n:, :]

    def measured(state):
        x, r, _, count = state
        x, r = advance(x, r)
        return x, r, row_norm(r), count + 1

    def bounded(state):
        x, r, bound = state
        return *advance(x, r), bound * bound

    def newton(_, x):
        return x + dot_split(x, unit - dot(scaled, x, precision=HIGHEST))

    x, r, bound, _ = lax.while_loop(
        lambda s: jnp.logical_and(s[2] > 0.95, s[3] < 40),
        measured,
        (x, r, jnp.where(far_off, 1.0, off * off), 0),
    )
    x, r, bound = lax.while_loop(lambda s: s[2] > 1e-7, bounded, (x, r, jnp.minimum(bound, 0.95)))
    x = lax.fori_loop(0, jnp.where(far_off, 4, jnp.where(off > 0.8, 1, 0)), newton, x)
    return x * scale_col * scale_row


def gram_of(context):
    return dot(context, context, ((0,), (0,)))


def gene_products(
    blocks, tensor_ref, factor_hbm, context_hbm, out_ref, keep, factor_ref, context_ref, left, sems, small
):
    depth = 3
    starts = [sum(blocks[:b]) for b in range(len(blocks))]
    copies = []
    for b, height in enumerate(blocks):
        rows = pl.ds(starts[b], height)
        copies.append(pltpu.make_async_copy(tensor_ref.at[rows, :], keep.at[rows, :], sems.at[b]))
    first = pltpu.make_async_copy(factor_hbm, factor_ref, small.at[0])
    second = pltpu.make_async_copy(context_hbm, context_ref, small.at[1])
    first.start()
    second.start()
    for copy in copies[:depth]:
        copy.start()
    contexts, rank = context_ref.shape
    chunks, tall, _ = out_ref.shape
    part = rank // chunks
    genes = tall - part
    first.wait()
    second.wait()
    context32 = context_ref[...].astype(f32)

    def build(b):
        perts = blocks[b] // contexts
        factor = factor_ref[pl.ds(starts[b] // contexts, perts), :].astype(f32)
        rows = (factor[:, None, :] * context32[None]).reshape(blocks[b], rank)
        hi, lo = split(rows.T)
        left[b % 2, :rank, : blocks[b]] = hi
        left[b % 2, rank:, : blocks[b]] = lo

    build(0)
    gram = gram_of(factor_ref[...])
    for q in range(chunks):
        out_ref[q, genes:, :] = gram[q * part : (q + 1) * part, :]
    total = None
    for b in range(len(blocks)):
        copies[b].wait()
        if b + depth < len(blocks):
            copies[b + depth].start()
        if b + 1 < len(blocks):
            build(b + 1)
        product = dot(left[b % 2, :, : blocks[b]], keep[pl.ds(starts[b], blocks[b]), :])
        total = product if total is None else total + product
    summed = (total[:rank, :] + total[rank:, :]).T
    for q in range(chunks):
        out_ref[q, :genes, :] = summed[q * genes : (q + 1) * genes, :]


def sum_and_copy(in_ref, out_ref):
    total = jnp.sum(in_ref[...], axis=0)
    for q in range(out_ref.shape[0]):
        out_ref[q] = total


def add(a_ref, b_ref, out_ref):
    out_ref[...] = a_ref[...] + b_ref[...]


def half_index():
    return lax.rem(lax.axis_index("gene"), 2)


def contract(blocks, core, tensor_ref, weights, context, gram_ref, out_ref):
    rank = gram_ref.shape[0]
    contexts = context.shape[0]
    context32 = context.astype(f32)
    half = tensor_ref.shape[0] // 2
    height = half // blocks
    per_block = height // contexts
    targets = out_ref.shape[0]
    perts = half // contexts // targets
    out_ref[:, perts:, :] = gram_ref[...].reshape(targets, rank // targets, rank)
    for b in range(blocks):
        start = pl.multiple_of(core * half + b * height, height)
        product = dot(tensor_ref[pl.ds(start, height), :], weights)
        wide = (product[:, :rank] + product[:, rank:]).reshape(per_block, contexts, rank)
        total = jnp.sum(wide * context32[None], axis=1)
        n = per_block // perts
        out_ref[pl.ds(b * n, n), :perts, :] = total.reshape(n, perts, rank)


def gene_solve(blocks, held_ref, context_ref, tensor_ref, other_ref, solved_ref, weights_ref, gram_ref):
    chunks, tall, rank = held_ref.shape
    genes = tall - rank // chunks
    context = context_ref[...]
    gram_a = jnp.concatenate([held_ref[q, genes:, :] for q in range(chunks)], axis=0)
    mttkrp = jnp.concatenate([held_ref[q, :genes, :] for q in range(chunks)], axis=0)
    inv = inverse(gram_a * gram_of(context))
    solved = dot(mttkrp, inv, precision=HIGHEST)
    solved_ref[...] = solved
    weights = jnp.concatenate(split(solved), axis=1)
    weights_ref[...] = weights
    product = dot(weights, weights, ((0,), (0,)))
    product = product[:, :rank] + product[:, rank:]
    gram_ref[...] = product[:rank, :] + product[rank:, :]
    contract(blocks, 1 - half_index(), tensor_ref, weights, context, gram_ref, other_ref)


def pert_products(blocks, weights_ref, context_ref, tensor_ref, gram_ref, mine_ref):
    contract(
        blocks, half_index(), tensor_ref, weights_ref[...], context_ref[...], gram_ref, mine_ref
    )


def pert_inverse(gene_count, mine_ref, context_ref, inv_ref, rate_ref):
    chunks, tall, rank = mine_ref.shape
    perts = tall - rank // chunks
    gram_s = mine_ref[:, perts:, :].reshape(rank, rank)
    diag_row, _ = diagonal(gram_s, eye(rank))
    scale_c = jnp.sqrt(diag_row / gene_count + epsilon)
    rate_ref[...] = 1.0 / scale_c
    inv_ref[...] = inverse(gram_s * gram_of(context_ref[...])) * scale_c


def gene_scale(solved_ref, rate_ref, out_ref):
    out_ref[...] = (solved_ref[...] * rate_ref[...]).astype(bf16)


def pert_solve(mine_ref, other_ref, inv_ref, out_ref, squares_ref):
    chunks, tall, rank = mine_ref.shape
    perts = tall - rank // chunks
    inv = inv_ref[...]
    mine = half_index()
    half = out_ref.shape[0] // 2
    squares = []
    for core, held_ref in ((mine, mine_ref), (1 - mine, other_ref)):
        mttkrp = held_ref[:, :perts, :].reshape(half, rank)
        solved = dot(mttkrp, inv, precision=HIGHEST)
        out_ref[pl.ds(pl.multiple_of(core * half, half), half), :] = solved
        squares.append(jnp.sum(solved * solved, axis=0, keepdims=True))
    squares_ref[...] = jnp.broadcast_to((squares[0] + squares[1])[None], squares_ref.shape)


def pert_scale(pert_count, held_ref, solved_ref, out_ref):
    squares = jnp.sum(held_ref[...], axis=0)
    scale_a = jnp.sqrt(squares / pert_count + epsilon)
    out_ref[...] = (solved_ref[...] * (1.0 / scale_a)).astype(bf16)


VMEM = pl.BlockSpec(memory_space=pltpu.VMEM)
FAR = pl.BlockSpec(memory_space=pltpu.HBM)


def near(x):
    return pltpu.with_memory_space_constraint(x, pltpu.VMEM)


def far(x):
    return pltpu.with_memory_space_constraint(x, pltpu.HBM)


def call(body, name, inputs, outputs, in_specs=None, scratch=(), limit=16):
    single = not isinstance(outputs, tuple)
    return pl.pallas_call(
        body,
        in_specs=in_specs or [VMEM] * len(inputs),
        out_specs=VMEM if single else (VMEM,) * len(outputs),
        out_shape=outputs,
        scratch_shapes=list(scratch),
        compiler_params=pltpu.CompilerParams(vmem_limit_bytes=limit << 20),
        name=name,
    )(*inputs)


def summed_copies(x, name):
    return call(sum_and_copy, name, (near(x),), pltpu.VMEM(x.shape, f32))


def shards(tensor, pert_factor, context_factor):
    rows_i, contexts, rows_j = tensor.shape
    rank = pert_factor.shape[1]
    n_pert = lax.axis_size("pert")
    n_gene = lax.axis_size("gene")
    flat = tensor.reshape(rows_i * contexts, rows_j)
    eighth = rows_i * contexts // 8
    blocks = (eighth, eighth, 2 * eighth, 2 * eighth, 2 * eighth)
    tall = rows_j // n_pert + rank // n_pert

    partial, kept = call(
        functools.partial(gene_products, blocks),
        "gene_products",
        (far(flat), far(pert_factor), far(context_factor)),
        (pltpu.VMEM((n_pert, tall, rank), f32), pltpu.VMEM(flat.shape, bf16)),
        in_specs=[FAR] * 3,
        scratch=(
            pltpu.VMEM(pert_factor.shape, bf16),
            pltpu.VMEM(context_factor.shape, bf16),
            pltpu.VMEM((2, 2 * rank, max(blocks)), bf16),
            pltpu.SemaphoreType.DMA((len(blocks),)),
            pltpu.SemaphoreType.DMA((2,)),
        ),
    )
    partial = lax.all_to_all(partial, "pert", 0, 0)
    gathered = lax.all_to_all(summed_copies(partial, "pert_sum"), "pert", 0, 0)

    context_factor = near(context_factor)
    chips = n_gene // 2
    perts = rows_i // n_gene
    message = pltpu.VMEM((chips, perts + rank // chips, rank), f32)
    square = pltpu.VMEM((rank, rank), f32)
    kept = near(kept)
    other, solved_c, weights, gram_s = call(
        functools.partial(gene_solve, 4),
        "gene_solve",
        (near(gathered), context_factor, kept),
        (
            message,
            pltpu.VMEM((rows_j, rank), f32),
            pltpu.VMEM((rows_j, 2 * rank), bf16),
            square,
        ),
    )
    swap = [(i, i ^ 1) for i in range(n_gene)]
    groups = [[2 * i + core for i in range(chips)] for core in range(2)]
    other = lax.ppermute(other, "gene", swap)
    mine = call(
        functools.partial(pert_products, 4),
        "pert_products",
        (near(weights), context_factor, kept, near(gram_s)),
        message,
    )
    partial = call(add, "core_sum", (near(mine), near(other)), message)
    partial = lax.all_to_all(partial, "gene", 0, 0, axis_index_groups=groups)
    mine = lax.all_to_all(
        summed_copies(partial, "gene_sum"), "gene", 0, 0, axis_index_groups=groups
    )
    other = lax.ppermute(mine, "gene", swap)
    mine = near(mine)
    inv, rate = call(
        functools.partial(pert_inverse, rows_j * n_gene),
        "pert_inverse",
        (mine, context_factor),
        (square, pltpu.VMEM((1, rank), f32)),
    )
    solved_a, squares = call(
        pert_solve,
        "pert_solve",
        (mine, near(other), near(inv)),
        (pltpu.VMEM((rows_i, rank), f32), pltpu.VMEM((n_pert, 1, rank), f32)),
    )
    squares = lax.all_to_all(squares, "pert", 0, 0)
    gene_factor = call(
        gene_scale,
        "gene_scale",
        (near(solved_c), near(rate)),
        jax.ShapeDtypeStruct((rows_j, rank), bf16),
    )
    pert_updated = call(
        functools.partial(pert_scale, rows_i * n_pert),
        "pert_scale",
        (near(squares), near(solved_a)),
        jax.ShapeDtypeStruct((rows_i, rank), bf16),
    )
    return (gene_factor, pert_updated)


def solution(mesh):
    return jax.shard_map(
        shards,
        mesh=mesh,
        in_specs=(P("pert", None, "gene"), P("pert", None), P()),
        out_specs=(P("gene", None), P("pert", None)),
        check_vma=False,
    )
```

```python
import functools

import jax
import jax.numpy as jnp
from jax import lax
from jax.experimental import pallas as pl
from jax.experimental.pallas import tpu as pltpu
from jax.sharding import PartitionSpec as P

epsilon = 1e-06
f32 = jnp.float32
bf16 = jnp.bfloat16
HIGHEST = lax.Precision.HIGHEST


def dot(a, b, dims=((1,), (0,)), precision=None):
    return lax.dot_general(a, b, (dims, ((), ())), precision=precision, preferred_element_type=f32)


def split(x):
    hi = x.astype(bf16)
    return hi, (x - hi.astype(f32)).astype(bf16)


def dot_split(a, b):
    n = b.shape[1]
    right = jnp.concatenate(split(b), axis=1)
    product = dot(jnp.concatenate(split(a), axis=1), jnp.concatenate([right, right], axis=0))
    return product[:, :n] + product[:, n:]


def eye(n):
    return (
        lax.broadcasted_iota(jnp.int32, (n, n), 0) == lax.broadcasted_iota(jnp.int32, (n, n), 1)
    ).astype(f32)


def diagonal(a, unit):
    picked = a * unit
    return jnp.sum(picked, axis=0, keepdims=True), jnp.sum(picked, axis=1, keepdims=True)


def row_norm(a):
    return jnp.max(jnp.sum(jnp.abs(a), axis=1, keepdims=True))


def inverse(a):
    unit = eye(a.shape[0])
    diag_row, diag_col = diagonal(a, unit)
    scale_row, scale_col = lax.rsqrt(diag_row), lax.rsqrt(diag_col)
    scaled = a * scale_col * scale_row
    off = row_norm(unit - scaled)
    far_off = off >= 0.95
    alpha = jnp.where(far_off, 1.0 / (1.0 + off), 1.0)
    r = unit - alpha * scaled
    x = alpha * (unit + r)
    r = dot_split(r, r)
    n = a.shape[0]

    def advance(x, r):
        product = dot_split(jnp.concatenate([x, r], axis=0), r)
        return x + product[:n, :], product[n:, :]

    def more(state):
        x, r, bound, count = state
        norm = row_norm(r)
        return *advance(x, r), norm * norm, count + 1

    def newton(_, x):
        return x + dot_split(x, unit - dot(scaled, x, precision=HIGHEST))

    x, r, bound, _ = lax.while_loop(
        lambda s: jnp.logical_and(s[2] > 1e-7, s[3] < 40),
        more,
        (x, r, jnp.where(far_off, 1.0, off * off), 0),
    )
    x = lax.fori_loop(0, jnp.where(far_off, 4, jnp.where(off > 0.8, 1, 0)), newton, x)
    return x * scale_col * scale_row


def gram_of(context):
    return dot(context, context, ((0,), (0,)))


def gene_products(
    blocks, tensor_ref, factor_hbm, context_hbm, out_ref, keep, factor_ref, context_ref, left, sems, small
):
    depth = 3
    starts = [sum(blocks[:b]) for b in range(len(blocks))]
    copies = []
    for b, height in enumerate(blocks):
        rows = pl.ds(starts[b], height)
        copies.append(pltpu.make_async_copy(tensor_ref.at[rows, :], keep.at[rows, :], sems.at[b]))
    first = pltpu.make_async_copy(factor_hbm, factor_ref, small.at[0])
    second = pltpu.make_async_copy(context_hbm, context_ref, small.at[1])
    first.start()
    second.start()
    for copy in copies[:depth]:
        copy.start()
    contexts, rank = context_ref.shape
    chunks, tall, _ = out_ref.shape
    part = rank // chunks
    genes = tall - part
    first.wait()
    second.wait()
    context32 = context_ref[...].astype(f32)

    def build(b):
        perts = blocks[b] // contexts
        factor = factor_ref[pl.ds(starts[b] // contexts, perts), :].astype(f32)
        rows = (factor[:, None, :] * context32[None]).reshape(blocks[b], rank)
        hi, lo = split(rows.T)
        left[b % 2, :rank, : blocks[b]] = hi
        left[b % 2, rank:, : blocks[b]] = lo

    build(0)
    gram = gram_of(factor_ref[...])
    for q in range(chunks):
        out_ref[q, genes:, :] = gram[q * part : (q + 1) * part, :]
    total = None
    for b in range(len(blocks)):
        copies[b].wait()
        if b + depth < len(blocks):
            copies[b + depth].start()
        if b + 1 < len(blocks):
            build(b + 1)
        product = dot(left[b % 2, :, : blocks[b]], keep[pl.ds(starts[b], blocks[b]), :])
        total = product if total is None else total + product
    summed = (total[:rank, :] + total[rank:, :]).T
    for q in range(chunks):
        out_ref[q, :genes, :] = summed[q * genes : (q + 1) * genes, :]


def sum_and_copy(in_ref, out_ref):
    total = jnp.sum(in_ref[...], axis=0)
    for q in range(out_ref.shape[0]):
        out_ref[q] = total


def add(a_ref, b_ref, out_ref):
    out_ref[...] = a_ref[...] + b_ref[...]


def half_index():
    return lax.rem(lax.axis_index("gene"), 2)


def contract(blocks, core, tensor_ref, weights, context, gram_ref, out_ref):
    rank = gram_ref.shape[0]
    contexts = context.shape[0]
    context32 = context.astype(f32)
    half = tensor_ref.shape[0] // 2
    height = half // blocks
    per_block = height // contexts
    targets = out_ref.shape[0]
    perts = half // contexts // targets
    out_ref[:, perts:, :] = gram_ref[...].reshape(targets, rank // targets, rank)
    for b in range(blocks):
        start = pl.multiple_of(core * half + b * height, height)
        product = dot(tensor_ref[pl.ds(start, height), :], weights)
        wide = (product[:, :rank] + product[:, rank:]).reshape(per_block, contexts, rank)
        total = jnp.sum(wide * context32[None], axis=1)
        n = per_block // perts
        out_ref[pl.ds(b * n, n), :perts, :] = total.reshape(n, perts, rank)


def gene_solve(blocks, held_ref, context_ref, tensor_ref, other_ref, solved_ref, weights_ref, gram_ref):
    chunks, tall, rank = held_ref.shape
    genes = tall - rank // chunks
    context = context_ref[...]
    gram_a = jnp.concatenate([held_ref[q, genes:, :] for q in range(chunks)], axis=0)
    mttkrp = jnp.concatenate([held_ref[q, :genes, :] for q in range(chunks)], axis=0)
    inv = inverse(gram_a * gram_of(context))
    solved = dot(mttkrp, inv, precision=HIGHEST)
    solved_ref[...] = solved
    weights = jnp.concatenate(split(solved), axis=1)
    weights_ref[...] = weights
    product = dot(weights, weights, ((0,), (0,)))
    product = product[:, :rank] + product[:, rank:]
    gram_ref[...] = product[:rank, :] + product[rank:, :]
    contract(blocks, 1 - half_index(), tensor_ref, weights, context, gram_ref, other_ref)


def pert_products(blocks, weights_ref, context_ref, tensor_ref, gram_ref, mine_ref):
    contract(
        blocks, half_index(), tensor_ref, weights_ref[...], context_ref[...], gram_ref, mine_ref
    )


def pert_inverse(gene_count, mine_ref, context_ref, inv_ref, rate_ref):
    chunks, tall, rank = mine_ref.shape
    perts = tall - rank // chunks
    gram_s = mine_ref[:, perts:, :].reshape(rank, rank)
    diag_row, _ = diagonal(gram_s, eye(rank))
    scale_c = jnp.sqrt(diag_row / gene_count + epsilon)
    rate_ref[...] = 1.0 / scale_c
    inv_ref[...] = inverse(gram_s * gram_of(context_ref[...])) * scale_c


def pert_solve(mine_ref, other_ref, inv_ref, out_ref, squares_ref):
    chunks, tall, rank = mine_ref.shape
    perts = tall - rank // chunks
    inv = inv_ref[...]
    mine = half_index()
    half = out_ref.shape[0] // 2
    squares = []
    for core, held_ref in ((mine, mine_ref), (1 - mine, other_ref)):
        mttkrp = held_ref[:, :perts, :].reshape(half, rank)
        solved = dot(mttkrp, inv, precision=HIGHEST)
        out_ref[pl.ds(pl.multiple_of(core * half, half), half), :] = solved
        squares.append(jnp.sum(solved * solved, axis=0, keepdims=True))
    squares_ref[...] = jnp.broadcast_to((squares[0] + squares[1])[None], squares_ref.shape)


def scale(pert_count, held_ref, solved_a_ref, solved_c_ref, rate_ref, gene_ref, pert_ref, gene, pert, sems):
    gene[...] = (solved_c_ref[...] * rate_ref[...]).astype(bf16)
    first = pltpu.make_async_copy(gene, gene_ref, sems.at[0])
    first.start()
    squares = jnp.sum(held_ref[...], axis=0)
    rate = 1.0 / jnp.sqrt(squares / pert_count + epsilon)
    half = pert.shape[0] // 2
    copies = []
    for h in range(2):
        rows = pl.ds(h * half, half)
        pert[rows, :] = (solved_a_ref[rows, :] * rate).astype(bf16)
        copy = pltpu.make_async_copy(pert.at[rows, :], pert_ref.at[rows, :], sems.at[1 + h])
        copy.start()
        copies.append(copy)
    first.wait()
    for copy in copies:
        copy.wait()


VMEM = pl.BlockSpec(memory_space=pltpu.VMEM)
FAR = pl.BlockSpec(memory_space=pltpu.HBM)


def near(x):
    return pltpu.with_memory_space_constraint(x, pltpu.VMEM)


def far(x):
    return pltpu.with_memory_space_constraint(x, pltpu.HBM)


def call(body, name, inputs, outputs, in_specs=None, out_spec=VMEM, scratch=(), limit=16):
    single = not isinstance(outputs, tuple)
    return pl.pallas_call(
        body,
        in_specs=in_specs or [VMEM] * len(inputs),
        out_specs=out_spec if single else (out_spec,) * len(outputs),
        out_shape=outputs,
        scratch_shapes=list(scratch),
        compiler_params=pltpu.CompilerParams(vmem_limit_bytes=limit << 20),
        name=name,
    )(*inputs)


def summed_copies(x, name):
    return call(sum_and_copy, name, (near(x),), pltpu.VMEM(x.shape, f32))


def shards(tensor, pert_factor, context_factor):
    rows_i, contexts, rows_j = tensor.shape
    rank = pert_factor.shape[1]
    n_pert = lax.axis_size("pert")
    n_gene = lax.axis_size("gene")
    flat = tensor.reshape(rows_i * contexts, rows_j)
    eighth = rows_i * contexts // 8
    blocks = (eighth, eighth, 2 * eighth, 2 * eighth, 2 * eighth)
    tall = rows_j // n_pert + rank // n_pert

    partial, kept = call(
        functools.partial(gene_products, blocks),
        "gene_products",
        (far(flat), far(pert_factor), far(context_factor)),
        (pltpu.VMEM((n_pert, tall, rank), f32), pltpu.VMEM(flat.shape, bf16)),
        in_specs=[FAR] * 3,
        scratch=(
            pltpu.VMEM(pert_factor.shape, bf16),
            pltpu.VMEM(context_factor.shape, bf16),
            pltpu.VMEM((2, 2 * rank, max(blocks)), bf16),
            pltpu.SemaphoreType.DMA((len(blocks),)),
            pltpu.SemaphoreType.DMA((2,)),
        ),
    )
    partial = lax.all_to_all(partial, "pert", 0, 0)
    gathered = lax.all_to_all(summed_copies(partial, "pert_sum"), "pert", 0, 0)

    context_factor = near(context_factor)
    chips = n_gene // 2
    perts = rows_i // n_gene
    message = pltpu.VMEM((chips, perts + rank // chips, rank), f32)
    square = pltpu.VMEM((rank, rank), f32)
    kept = near(kept)
    other, solved_c, weights, gram_s = call(
        functools.partial(gene_solve, 4),
        "gene_solve",
        (near(gathered), context_factor, kept),
        (
            message,
            pltpu.VMEM((rows_j, rank), f32),
            pltpu.VMEM((rows_j, 2 * rank), bf16),
            square,
        ),
    )
    swap = [(i, i ^ 1) for i in range(n_gene)]
    groups = [[2 * i + core for i in range(chips)] for core in range(2)]
    other = lax.ppermute(other, "gene", swap)
    mine = call(
        functools.partial(pert_products, 4),
        "pert_products",
        (near(weights), context_factor, kept, near(gram_s)),
        message,
    )
    partial = call(add, "core_sum", (near(mine), near(other)), message)
    partial = lax.all_to_all(partial, "gene", 0, 0, axis_index_groups=groups)
    mine = lax.all_to_all(
        summed_copies(partial, "gene_sum"), "gene", 0, 0, axis_index_groups=groups
    )
    other = lax.ppermute(mine, "gene", swap)
    mine = near(mine)
    inv, rate = call(
        functools.partial(pert_inverse, rows_j * n_gene),
        "pert_inverse",
        (mine, context_factor),
        (square, pltpu.VMEM((1, rank), f32)),
    )
    solved_a, squares = call(
        pert_solve,
        "pert_solve",
        (mine, near(other), near(inv)),
        (pltpu.VMEM((rows_i, rank), f32), pltpu.VMEM((n_pert, 1, rank), f32)),
    )
    squares = lax.all_to_all(squares, "pert", 0, 0)
    outputs = (
        jax.ShapeDtypeStruct((rows_j, rank), bf16),
        jax.ShapeDtypeStruct((rows_i, rank), bf16),
    )
    return call(
        functools.partial(scale, rows_i * n_pert),
        "scale",
        (near(squares), near(solved_a), near(solved_c), near(rate)),
        outputs,
        out_spec=FAR,
        scratch=[pltpu.VMEM(o.shape, bf16) for o in outputs] + [pltpu.SemaphoreType.DMA((3,))],
    )


def solution(mesh):
    return jax.shard_map(
        shards,
        mesh=mesh,
        in_specs=(P("pert", None, "gene"), P("pert", None), P()),
        out_specs=(P("gene", None), P("pert", None)),
        check_vma=False,
    )
```

```python
import functools

import jax
import jax.numpy as jnp
from jax import lax
from jax.experimental import pallas as pl
from jax.experimental.pallas import tpu as pltpu
from jax.sharding import PartitionSpec as P

epsilon = 1e-06
f32 = jnp.float32
bf16 = jnp.bfloat16
HIGHEST = lax.Precision.HIGHEST


def dot(a, b, dims=((1,), (0,)), precision=None):
    return lax.dot_general(a, b, (dims, ((), ())), precision=precision, preferred_element_type=f32)


def split(x):
    hi = x.astype(bf16)
    return hi, (x - hi.astype(f32)).astype(bf16)


def dot_split(a, b):
    n = b.shape[1]
    right = jnp.concatenate(split(b), axis=1)
    product = dot(jnp.concatenate(split(a), axis=1), jnp.concatenate([right, right], axis=0))
    return product[:, :n] + product[:, n:]


def eye(n):
    return (
        lax.broadcasted_iota(jnp.int32, (n, n), 0) == lax.broadcasted_iota(jnp.int32, (n, n), 1)
    ).astype(f32)


def diagonal(a, unit):
    picked = a * unit
    return jnp.sum(picked, axis=0, keepdims=True), jnp.sum(picked, axis=1, keepdims=True)


def row_norm(a):
    return jnp.max(jnp.sum(jnp.abs(a), axis=1, keepdims=True))


def inverse(a):
    unit = eye(a.shape[0])
    diag_row, diag_col = diagonal(a, unit)
    scale_row, scale_col = lax.rsqrt(diag_row), lax.rsqrt(diag_col)
    scaled = a * scale_col * scale_row
    off = row_norm(unit - scaled)
    far_off = off >= 0.95
    alpha = jnp.where(far_off, 1.0 / (1.0 + off), 1.0)
    r = unit - alpha * scaled
    x = alpha * (unit + r)
    r = dot_split(r, r)
    n = a.shape[0]

    def advance(x, r):
        product = dot_split(jnp.concatenate([x, r], axis=0), r)
        return x + product[:n, :], product[n:, :]

    def more(state):
        x, r, bound, count = state
        norm = row_norm(r)
        return *advance(x, r), norm * norm, count + 1

    def newton(_, x):
        return x + dot_split(x, unit - dot(scaled, x, precision=HIGHEST))

    x, r, bound, _ = lax.while_loop(
        lambda s: jnp.logical_and(s[2] > 1e-7, s[3] < 40),
        more,
        (x, r, jnp.where(far_off, 1.0, off * off), 0),
    )
    x = lax.fori_loop(0, jnp.where(far_off, 4, jnp.where(off > 0.8, 1, 0)), newton, x)
    return x * scale_col * scale_row


def gram_of(context):
    return dot(context, context, ((0,), (0,)))


def gene_products(
    blocks, tensor_ref, factor_hbm, context_hbm, out_ref, keep, factor_ref, context_ref, left, sems, small
):
    depth = 3
    starts = [sum(blocks[:b]) for b in range(len(blocks))]
    copies = []
    for b, height in enumerate(blocks):
        rows = pl.ds(starts[b], height)
        copies.append(pltpu.make_async_copy(tensor_ref.at[rows, :], keep.at[rows, :], sems.at[b]))
    first = pltpu.make_async_copy(factor_hbm, factor_ref, small.at[0])
    second = pltpu.make_async_copy(context_hbm, context_ref, small.at[1])
    first.start()
    second.start()
    for copy in copies[:depth]:
        copy.start()
    contexts, rank = context_ref.shape
    chunks, tall, _ = out_ref.shape
    part = rank // chunks
    genes = tall - 2 * part
    first.wait()
    second.wait()
    context32 = context_ref[...].astype(f32)

    def build(b):
        perts = blocks[b] // contexts
        factor = factor_ref[pl.ds(starts[b] // contexts, perts), :].astype(f32)
        rows = (factor[:, None, :] * context32[None]).reshape(blocks[b], rank)
        hi, lo = split(rows.T)
        left[b % 2, :rank, : blocks[b]] = hi
        left[b % 2, rank:, : blocks[b]] = lo

    build(0)
    for shift, gram in enumerate(split(gram_of(factor_ref[...]))):
        for q in range(chunks):
            rows = pl.ds(genes + shift * part, part)
            out_ref[q, rows, :] = gram[q * part : (q + 1) * part, :]
    total = None
    for b in range(len(blocks)):
        copies[b].wait()
        if b + depth < len(blocks):
            copies[b + depth].start()
        if b + 1 < len(blocks):
            build(b + 1)
        product = dot(left[b % 2, :, : blocks[b]], keep[pl.ds(starts[b], blocks[b]), :])
        total = product if total is None else total + product
    summed = (total[:rank, :] + total[rank:, :]).T.astype(bf16)
    for q in range(chunks):
        out_ref[q, :genes, :] = summed[q * genes : (q + 1) * genes, :]


def sum_and_copy(in_ref, out_ref):
    total = jnp.sum(in_ref[...], axis=0)
    for q in range(out_ref.shape[0]):
        out_ref[q] = total


def narrow_sum_and_copy(part, in_ref, out_ref):
    total = jnp.sum(in_ref[...].astype(f32), axis=0)
    genes = total.shape[0] - 2 * part
    hi, lo = split(total[genes : genes + part, :] + total[genes + part :, :])
    total = jnp.concatenate([total[:genes, :].astype(bf16), hi, lo], axis=0)
    for q in range(out_ref.shape[0]):
        out_ref[q] = total


def add(a_ref, b_ref, out_ref):
    out_ref[...] = a_ref[...] + b_ref[...]


def half_index():
    return lax.rem(lax.axis_index("gene"), 2)


def contract(blocks, core, tensor_ref, weights, context, gram_ref, out_ref):
    rank = gram_ref.shape[0]
    contexts = context.shape[0]
    context32 = context.astype(f32)
    half = tensor_ref.shape[0] // 2
    height = half // blocks
    per_block = height // contexts
    targets = out_ref.shape[0]
    perts = half // contexts // targets
    out_ref[:, perts:, :] = gram_ref[...].reshape(targets, rank // targets, rank)
    for b in range(blocks):
        start = pl.multiple_of(core * half + b * height, height)
        product = dot(tensor_ref[pl.ds(start, height), :], weights)
        wide = (product[:, :rank] + product[:, rank:]).reshape(per_block, contexts, rank)
        total = jnp.sum(wide * context32[None], axis=1)
        n = per_block // perts
        out_ref[pl.ds(b * n, n), :perts, :] = total.reshape(n, perts, rank)


def gene_solve(blocks, held_ref, context_ref, tensor_ref, other_ref, solved_ref, weights_ref, gram_ref):
    chunks, tall, rank = held_ref.shape
    part = rank // chunks
    genes = tall - 2 * part
    context = context_ref[...]
    held = held_ref[...].astype(f32)
    gram_a = (held[:, genes : genes + part, :] + held[:, genes + part :, :]).reshape(rank, rank)
    mttkrp = held[:, :genes, :].reshape(chunks * genes, rank)
    inv = inverse(gram_a * gram_of(context))
    solved = dot(mttkrp, inv, precision=HIGHEST)
    solved_ref[...] = solved
    weights = jnp.concatenate(split(solved), axis=1)
    weights_ref[...] = weights
    product = dot(weights, weights, ((0,), (0,)))
    product = product[:, :rank] + product[:, rank:]
    gram_ref[...] = product[:rank, :] + product[rank:, :]
    contract(blocks, 1 - half_index(), tensor_ref, weights, context, gram_ref, other_ref)


def pert_products(blocks, weights_ref, context_ref, tensor_ref, gram_ref, mine_ref):
    contract(
        blocks, half_index(), tensor_ref, weights_ref[...], context_ref[...], gram_ref, mine_ref
    )


def pert_inverse(gene_count, mine_ref, context_ref, inv_ref, rate_ref):
    chunks, tall, rank = mine_ref.shape
    perts = tall - rank // chunks
    gram_s = mine_ref[:, perts:, :].reshape(rank, rank)
    diag_row, _ = diagonal(gram_s, eye(rank))
    scale_c = jnp.sqrt(diag_row / gene_count + epsilon)
    rate_ref[...] = 1.0 / scale_c
    inv_ref[...] = inverse(gram_s * gram_of(context_ref[...])) * scale_c


def pert_solve(mine_ref, other_ref, inv_ref, out_ref, squares_ref):
    chunks, tall, rank = mine_ref.shape
    perts = tall - rank // chunks
    inv = inv_ref[...]
    mine = half_index()
    half = out_ref.shape[0] // 2
    squares = []
    for core, held_ref in ((mine, mine_ref), (1 - mine, other_ref)):
        mttkrp = held_ref[:, :perts, :].reshape(half, rank)
        solved = dot(mttkrp, inv, precision=HIGHEST)
        out_ref[pl.ds(pl.multiple_of(core * half, half), half), :] = solved
        squares.append(jnp.sum(solved * solved, axis=0, keepdims=True))
    squares_ref[...] = jnp.broadcast_to((squares[0] + squares[1])[None], squares_ref.shape)


def scale(pert_count, held_ref, solved_a_ref, solved_c_ref, rate_ref, gene_ref, pert_ref, gene, pert, sems):
    gene[...] = (solved_c_ref[...] * rate_ref[...]).astype(bf16)
    first = pltpu.make_async_copy(gene, gene_ref, sems.at[0])
    first.start()
    squares = jnp.sum(held_ref[...], axis=0)
    rate = 1.0 / jnp.sqrt(squares / pert_count + epsilon)
    half = pert.shape[0] // 2
    copies = []
    for h in range(2):
        rows = pl.ds(h * half, half)
        pert[rows, :] = (solved_a_ref[rows, :] * rate).astype(bf16)
        copy = pltpu.make_async_copy(pert.at[rows, :], pert_ref.at[rows, :], sems.at[1 + h])
        copy.start()
        copies.append(copy)
    first.wait()
    for copy in copies:
        copy.wait()


VMEM = pl.BlockSpec(memory_space=pltpu.VMEM)
FAR = pl.BlockSpec(memory_space=pltpu.HBM)


def near(x):
    return pltpu.with_memory_space_constraint(x, pltpu.VMEM)


def far(x):
    return pltpu.with_memory_space_constraint(x, pltpu.HBM)


def call(body, name, inputs, outputs, in_specs=None, out_spec=VMEM, scratch=(), limit=16):
    single = not isinstance(outputs, tuple)
    return pl.pallas_call(
        body,
        in_specs=in_specs or [VMEM] * len(inputs),
        out_specs=out_spec if single else (out_spec,) * len(outputs),
        out_shape=outputs,
        scratch_shapes=list(scratch),
        compiler_params=pltpu.CompilerParams(vmem_limit_bytes=limit << 20),
        name=name,
    )(*inputs)


def summed_copies(body, x, name):
    return call(body, name, (near(x),), pltpu.VMEM(x.shape, x.dtype))


def shards(tensor, pert_factor, context_factor):
    rows_i, contexts, rows_j = tensor.shape
    rank = pert_factor.shape[1]
    n_pert = lax.axis_size("pert")
    n_gene = lax.axis_size("gene")
    flat = tensor.reshape(rows_i * contexts, rows_j)
    eighth = rows_i * contexts // 8
    blocks = (eighth, eighth, 2 * eighth, 2 * eighth, 2 * eighth)
    part = rank // n_pert
    tall = rows_j // n_pert + 2 * part

    partial, kept = call(
        functools.partial(gene_products, blocks),
        "gene_products",
        (far(flat), far(pert_factor), far(context_factor)),
        (pltpu.VMEM((n_pert, tall, rank), bf16), pltpu.VMEM(flat.shape, bf16)),
        in_specs=[FAR] * 3,
        scratch=(
            pltpu.VMEM(pert_factor.shape, bf16),
            pltpu.VMEM(context_factor.shape, bf16),
            pltpu.VMEM((2, 2 * rank, max(blocks)), bf16),
            pltpu.SemaphoreType.DMA((len(blocks),)),
            pltpu.SemaphoreType.DMA((2,)),
        ),
    )
    partial = lax.all_to_all(partial, "pert", 0, 0)
    gathered = lax.all_to_all(
        summed_copies(functools.partial(narrow_sum_and_copy, part), partial, "pert_sum"), "pert", 0, 0
    )

    context_factor = near(context_factor)
    chips = n_gene // 2
    perts = rows_i // n_gene
    message = pltpu.VMEM((chips, perts + rank // chips, rank), f32)
    square = pltpu.VMEM((rank, rank), f32)
    kept = near(kept)
    other, solved_c, weights, gram_s = call(
        functools.partial(gene_solve, 4),
        "gene_solve",
        (near(gathered), context_factor, kept),
        (
            message,
            pltpu.VMEM((rows_j, rank), f32),
            pltpu.VMEM((rows_j, 2 * rank), bf16),
            square,
        ),
    )
    swap = [(i, i ^ 1) for i in range(n_gene)]
    groups = [[2 * i + core for i in range(chips)] for core in range(2)]
    other = lax.ppermute(other, "gene", swap)
    mine = call(
        functools.partial(pert_products, 4),
        "pert_products",
        (near(weights), context_factor, kept, near(gram_s)),
        message,
    )
    partial = call(add, "core_sum", (near(mine), near(other)), message)
    partial = lax.all_to_all(partial, "gene", 0, 0, axis_index_groups=groups)
    mine = lax.all_to_all(
        summed_copies(sum_and_copy, partial, "gene_sum"), "gene", 0, 0, axis_index_groups=groups
    )
    other = lax.ppermute(mine, "gene", swap)
    mine = near(mine)
    inv, rate = call(
        functools.partial(pert_inverse, rows_j * n_gene),
        "pert_inverse",
        (mine, context_factor),
        (square, pltpu.VMEM((1, rank), f32)),
    )
    solved_a, squares = call(
        pert_solve,
        "pert_solve",
        (mine, near(other), near(inv)),
        (pltpu.VMEM((rows_i, rank), f32), pltpu.VMEM((n_pert, 1, rank), f32)),
    )
    squares = lax.all_to_all(squares, "pert", 0, 0)
    outputs = (
        jax.ShapeDtypeStruct((rows_j, rank), bf16),
        jax.ShapeDtypeStruct((rows_i, rank), bf16),
    )
    return call(
        functools.partial(scale, rows_i * n_pert),
        "scale",
        (near(squares), near(solved_a), near(solved_c), near(rate)),
        outputs,
        out_spec=FAR,
        scratch=[pltpu.VMEM(o.shape, bf16) for o in outputs] + [pltpu.SemaphoreType.DMA((3,))],
    )


def solution(mesh):
    return jax.shard_map(
        shards,
        mesh=mesh,
        in_specs=(P("pert", None, "gene"), P("pert", None), P()),
        out_specs=(P("gene", None), P("pert", None)),
        check_vma=False,
    )
```

```python
import functools

import jax
import jax.numpy as jnp
from jax import lax
from jax.experimental import pallas as pl
from jax.experimental.pallas import tpu as pltpu
from jax.sharding import PartitionSpec as P

epsilon = 1e-06
f32 = jnp.float32
bf16 = jnp.bfloat16
HIGHEST = lax.Precision.HIGHEST


def dot(a, b, dims=((1,), (0,)), precision=None):
    return lax.dot_general(a, b, (dims, ((), ())), precision=precision, preferred_element_type=f32)


def split(x):
    hi = x.astype(bf16)
    return hi, (x - hi.astype(f32)).astype(bf16)


def dot_split(a, b):
    n = b.shape[1]
    right = jnp.concatenate(split(b), axis=1)
    product = dot(jnp.concatenate(split(a), axis=1), jnp.concatenate([right, right], axis=0))
    return product[:, :n] + product[:, n:]


def eye(n):
    return (
        lax.broadcasted_iota(jnp.int32, (n, n), 0) == lax.broadcasted_iota(jnp.int32, (n, n), 1)
    ).astype(f32)


def diagonal(a, unit):
    picked = a * unit
    return jnp.sum(picked, axis=0, keepdims=True), jnp.sum(picked, axis=1, keepdims=True)


def row_norm(a):
    return jnp.max(jnp.sum(jnp.abs(a), axis=1, keepdims=True))


def inverse(a):
    unit = eye(a.shape[0])
    diag_row, diag_col = diagonal(a, unit)
    scale_row, scale_col = lax.rsqrt(diag_row), lax.rsqrt(diag_col)
    scaled = a * scale_col * scale_row
    off = row_norm(unit - scaled)
    far_off = off >= 0.95
    alpha = jnp.where(far_off, 1.0 / (1.0 + off), 1.0)
    r = unit - alpha * scaled
    x = alpha * (unit + r)
    r = dot_split(r, r)
    n = a.shape[0]

    def advance(x, r):
        product = dot_split(jnp.concatenate([x, r], axis=0), r)
        return x + product[:n, :], product[n:, :]

    def more(state):
        x, r, bound, count = state
        norm = row_norm(r)
        return *advance(x, r), norm * norm, count + 1

    def newton(_, x):
        return x + dot_split(x, unit - dot(scaled, x, precision=HIGHEST))

    x, r, bound, _ = lax.while_loop(
        lambda s: jnp.logical_and(s[2] > 1e-7, s[3] < 40),
        more,
        (x, r, jnp.where(far_off, 1.0, off * off), 0),
    )
    x = lax.fori_loop(0, jnp.where(far_off, 4, jnp.where(off > 0.8, 1, 0)), newton, x)
    return x * scale_col * scale_row


def gram_of(context):
    return dot(context, context, ((0,), (0,)))


def gene_products(
    blocks, tensor_ref, factor_hbm, context_hbm, out_ref, keep, factor_ref, context_ref, left, sems, small
):
    depth = 3
    starts = [sum(blocks[:b]) for b in range(len(blocks))]
    copies = []
    for b, height in enumerate(blocks):
        rows = pl.ds(starts[b], height)
        copies.append(pltpu.make_async_copy(tensor_ref.at[rows, :], keep.at[rows, :], sems.at[b]))
    first = pltpu.make_async_copy(factor_hbm, factor_ref, small.at[0])
    second = pltpu.make_async_copy(context_hbm, context_ref, small.at[1])
    first.start()
    second.start()
    for copy in copies[:depth]:
        copy.start()
    contexts, rank = context_ref.shape
    chunks, tall, _ = out_ref.shape
    part = rank // chunks
    genes = tall - 2 * part
    first.wait()
    second.wait()
    context32 = context_ref[...].astype(f32)

    def build(b):
        perts = blocks[b] // contexts
        factor = factor_ref[pl.ds(starts[b] // contexts, perts), :].astype(f32)
        rows = (factor[:, None, :] * context32[None]).reshape(blocks[b], rank)
        hi, lo = split(rows.T)
        left[b % 2, :rank, : blocks[b]] = hi
        left[b % 2, rank:, : blocks[b]] = lo

    build(0)
    for shift, gram in enumerate(split(gram_of(factor_ref[...]))):
        for q in range(chunks):
            rows = pl.ds(genes + shift * part, part)
            out_ref[q, rows, :] = gram[q * part : (q + 1) * part, :]
    total = None
    for b in range(len(blocks)):
        copies[b].wait()
        if b + depth < len(blocks):
            copies[b + depth].start()
        if b + 1 < len(blocks):
            build(b + 1)
        product = dot(left[b % 2, :, : blocks[b]], keep[pl.ds(starts[b], blocks[b]), :])
        total = product if total is None else total + product
    summed = (total[:rank, :] + total[rank:, :]).T.astype(bf16)
    for q in range(chunks):
        out_ref[q, :genes, :] = summed[q * genes : (q + 1) * genes, :]


def narrow_sum_and_copy(part, in_ref, out_ref):
    total = jnp.sum(in_ref[...].astype(f32), axis=0)
    genes = total.shape[0] - 2 * part
    hi, lo = split(total[genes : genes + part, :] + total[genes + part :, :])
    total = jnp.concatenate([total[:genes, :].astype(bf16), hi, lo], axis=0)
    for q in range(out_ref.shape[0]):
        out_ref[q] = total


def half_index():
    return lax.rem(lax.axis_index("gene"), 2)


def gene_solve(blocks, held_ref, context_ref, tensor_ref, out_ref, solved_ref):
    chunks, tall, rank = held_ref.shape
    part = rank // chunks
    genes = tall - 2 * part
    context = context_ref[...]
    held = held_ref[...].astype(f32)
    gram_a = (held[:, genes : genes + part, :] + held[:, genes + part :, :]).reshape(rank, rank)
    mttkrp = held[:, :genes, :].reshape(chunks * genes, rank)
    inv = inverse(gram_a * gram_of(context))
    solved = dot(mttkrp, inv, precision=HIGHEST)
    solved_ref[...] = solved
    weights = jnp.concatenate(split(solved), axis=1)
    product = dot(weights, weights, ((0,), (0,)))
    product = product[:, :rank] + product[:, rank:]
    high, low = (x.astype(f32) for x in split(product[:rank, :] + product[rank:, :]))
    targets = out_ref.shape[0]
    share = rank // targets
    contexts = context.shape[0]
    perts = tensor_ref.shape[0] // contexts // targets
    for q in range(targets):
        rows = slice(q * share, (q + 1) * share)
        out_ref[q, perts:, :] = jnp.concatenate([high[rows, :], low[rows, :]], axis=0).astype(bf16)
    context32 = context.astype(f32)
    height = tensor_ref.shape[0] // blocks
    per_block = height // contexts
    chips = targets // 2
    for b in range(blocks):
        product = dot(tensor_ref[pl.ds(b * height, height), :], weights)
        wide = (product[:, :rank] + product[:, rank:]).reshape(per_block, contexts, rank)
        total = jnp.sum(wide * context32[None], axis=1).astype(bf16)
        for n in range(per_block // perts):
            core, chip = divmod(b * per_block // perts + n, chips)
            out_ref[2 * chip + core, :perts, :] = total[n * perts : (n + 1) * perts, :]


def gene_sum(share, in_ref, out_ref):
    total = jnp.sum(in_ref[...].astype(f32), axis=0)
    perts = total.shape[0] - 2 * share
    gram = total[perts : perts + share, :] + total[perts + share :, :]
    none = jnp.zeros_like(gram)
    gram = jnp.where(
        half_index() == 0,
        jnp.concatenate([gram, none], axis=0),
        jnp.concatenate([none, gram], axis=0),
    )
    total = jnp.concatenate([total[:perts, :], gram], axis=0)
    for q in range(out_ref.shape[0]):
        out_ref[q] = total


def pert_solve(gene_count, mine_ref, other_ref, context_ref, out_ref, squares_ref, rate_ref):
    chunks, tall, rank = mine_ref.shape
    perts = tall - rank // chunks
    gram_s = (mine_ref[:, perts:, :] + other_ref[:, perts:, :]).reshape(rank, rank)
    diag_row, _ = diagonal(gram_s, eye(rank))
    scale_c = jnp.sqrt(diag_row / gene_count + epsilon)
    rate_ref[...] = 1.0 / scale_c
    inv = inverse(gram_s * gram_of(context_ref[...])) * scale_c
    mine = half_index()
    half = out_ref.shape[0] // 2
    squares = []
    for core, held_ref in ((mine, mine_ref), (1 - mine, other_ref)):
        mttkrp = held_ref[:, :perts, :].reshape(half, rank)
        solved = dot(mttkrp, inv, precision=HIGHEST)
        out_ref[pl.ds(pl.multiple_of(core * half, half), half), :] = solved
        squares.append(jnp.sum(solved * solved, axis=0, keepdims=True))
    squares_ref[...] = jnp.broadcast_to((squares[0] + squares[1])[None], squares_ref.shape)


def scale(pert_count, held_ref, solved_a_ref, solved_c_ref, rate_ref, gene_ref, pert_ref, gene, pert, sems):
    gene[...] = (solved_c_ref[...] * rate_ref[...]).astype(bf16)
    first = pltpu.make_async_copy(gene, gene_ref, sems.at[0])
    first.start()
    squares = jnp.sum(held_ref[...], axis=0)
    rate = 1.0 / jnp.sqrt(squares / pert_count + epsilon)
    half = pert.shape[0] // 2
    copies = []
    for h in range(2):
        rows = pl.ds(h * half, half)
        pert[rows, :] = (solved_a_ref[rows, :] * rate).astype(bf16)
        copy = pltpu.make_async_copy(pert.at[rows, :], pert_ref.at[rows, :], sems.at[1 + h])
        copy.start()
        copies.append(copy)
    first.wait()
    for copy in copies:
        copy.wait()


VMEM = pl.BlockSpec(memory_space=pltpu.VMEM)
FAR = pl.BlockSpec(memory_space=pltpu.HBM)


def near(x):
    return pltpu.with_memory_space_constraint(x, pltpu.VMEM)


def far(x):
    return pltpu.with_memory_space_constraint(x, pltpu.HBM)


def call(body, name, inputs, outputs, in_specs=None, out_spec=VMEM, scratch=(), limit=16):
    single = not isinstance(outputs, tuple)
    return pl.pallas_call(
        body,
        in_specs=in_specs or [VMEM] * len(inputs),
        out_specs=out_spec if single else (out_spec,) * len(outputs),
        out_shape=outputs,
        scratch_shapes=list(scratch),
        compiler_params=pltpu.CompilerParams(vmem_limit_bytes=limit << 20),
        name=name,
    )(*inputs)


def shards(tensor, pert_factor, context_factor):
    rows_i, contexts, rows_j = tensor.shape
    rank = pert_factor.shape[1]
    n_pert = lax.axis_size("pert")
    n_gene = lax.axis_size("gene")
    flat = tensor.reshape(rows_i * contexts, rows_j)
    eighth = rows_i * contexts // 8
    blocks = (eighth, eighth, 2 * eighth, 2 * eighth, 2 * eighth)
    part = rank // n_pert
    tall = rows_j // n_pert + 2 * part

    partial, kept = call(
        functools.partial(gene_products, blocks),
        "gene_products",
        (far(flat), far(pert_factor), far(context_factor)),
        (pltpu.VMEM((n_pert, tall, rank), bf16), pltpu.VMEM(flat.shape, bf16)),
        in_specs=[FAR] * 3,
        scratch=(
            pltpu.VMEM(pert_factor.shape, bf16),
            pltpu.VMEM(context_factor.shape, bf16),
            pltpu.VMEM((2, 2 * rank, max(blocks)), bf16),
            pltpu.SemaphoreType.DMA((len(blocks),)),
            pltpu.SemaphoreType.DMA((2,)),
        ),
    )
    partial = lax.all_to_all(partial, "pert", 0, 0)
    gathered = call(
        functools.partial(narrow_sum_and_copy, part),
        "pert_sum",
        (near(partial),),
        pltpu.VMEM(partial.shape, bf16),
    )
    gathered = lax.all_to_all(gathered, "pert", 0, 0)

    context_factor = near(context_factor)
    chips = n_gene // 2
    perts = rows_i // n_gene
    share = rank // n_gene
    partial, solved_c = call(
        functools.partial(gene_solve, 8),
        "gene_solve",
        (near(gathered), context_factor, near(kept)),
        (
            pltpu.VMEM((n_gene, perts + 2 * share, rank), bf16),
            pltpu.VMEM((rows_j, rank), f32),
        ),
    )
    partial = lax.all_to_all(partial, "gene", 0, 0)
    summed = call(
        functools.partial(gene_sum, share),
        "gene_sum",
        (near(partial),),
        pltpu.VMEM((chips, perts + 2 * share, rank), f32),
    )
    groups = [[2 * i + core for i in range(chips)] for core in range(2)]
    mine = lax.all_to_all(summed, "gene", 0, 0, axis_index_groups=groups)
    other = lax.ppermute(mine, "gene", [(i, i ^ 1) for i in range(n_gene)])
    solved_a, squares, rate = call(
        functools.partial(pert_solve, rows_j * n_gene),
        "pert_solve",
        (near(mine), near(other), context_factor),
        (
            pltpu.VMEM((rows_i, rank), f32),
            pltpu.VMEM((n_pert, 1, rank), f32),
            pltpu.VMEM((1, rank), f32),
        ),
    )
    squares = lax.all_to_all(squares, "pert", 0, 0)
    outputs = (
        jax.ShapeDtypeStruct((rows_j, rank), bf16),
        jax.ShapeDtypeStruct((rows_i, rank), bf16),
    )
    return call(
        functools.partial(scale, rows_i * n_pert),
        "scale",
        (near(squares), near(solved_a), near(solved_c), near(rate)),
        outputs,
        out_spec=FAR,
        scratch=[pltpu.VMEM(o.shape, bf16) for o in outputs] + [pltpu.SemaphoreType.DMA((3,))],
    )


def solution(mesh):
    return jax.shard_map(
        shards,
        mesh=mesh,
        in_specs=(P("pert", None, "gene"), P("pert", None), P()),
        out_specs=(P("gene", None), P("pert", None)),
        check_vma=False,
    )
```

```python
import functools

import jax
import jax.numpy as jnp
from jax import lax
from jax.experimental import pallas as pl
from jax.experimental.pallas import tpu as pltpu
from jax.sharding import PartitionSpec as P

epsilon = 1e-06
f32 = jnp.float32
bf16 = jnp.bfloat16
HIGHEST = lax.Precision.HIGHEST


def dot(a, b, dims=((1,), (0,)), precision=None):
    return lax.dot_general(a, b, (dims, ((), ())), precision=precision, preferred_element_type=f32)


def split(x):
    hi = x.astype(bf16)
    return hi, (x - hi.astype(f32)).astype(bf16)


def dot_split(a, b):
    n = b.shape[1]
    right = jnp.concatenate(split(b), axis=1)
    product = dot(jnp.concatenate(split(a), axis=1), jnp.concatenate([right, right], axis=0))
    return product[:, :n] + product[:, n:]


def eye(n):
    return (
        lax.broadcasted_iota(jnp.int32, (n, n), 0) == lax.broadcasted_iota(jnp.int32, (n, n), 1)
    ).astype(f32)


def diagonal(a, unit):
    picked = a * unit
    return jnp.sum(picked, axis=0, keepdims=True), jnp.sum(picked, axis=1, keepdims=True)


def row_norm(a):
    return jnp.max(jnp.sum(jnp.abs(a), axis=1, keepdims=True))


def inverse(a):
    unit = eye(a.shape[0])
    diag_row, diag_col = diagonal(a, unit)
    scale_row, scale_col = lax.rsqrt(diag_row), lax.rsqrt(diag_col)
    scaled = a * scale_col * scale_row
    off = row_norm(unit - scaled)
    far_off = off >= 0.95
    alpha = jnp.where(far_off, 1.0 / (1.0 + off), 1.0)
    r = unit - alpha * scaled
    x = alpha * (unit + r)
    r = dot_split(r, r)
    n = a.shape[0]

    def advance(x, r):
        product = dot_split(jnp.concatenate([x, r], axis=0), r)
        return x + product[:n, :], product[n:, :]

    def more(state):
        x, r, bound, count = state
        norm = row_norm(r)
        return *advance(x, r), norm * norm, count + 1

    def newton(_, x):
        return x + dot_split(x, unit - dot(scaled, x, precision=HIGHEST))

    x, r, bound, _ = lax.while_loop(
        lambda s: jnp.logical_and(s[2] > 1e-7, s[3] < 40),
        more,
        (x, r, jnp.where(far_off, 1.0, off * off), 0),
    )
    x = lax.fori_loop(0, jnp.where(far_off, 4, jnp.where(off > 0.8, 1, 0)), newton, x)
    return x * scale_col * scale_row


def gram_of(context):
    return dot(context, context, ((0,), (0,)))


def gene_products(
    blocks, tensor_ref, factor_hbm, context_hbm, out_ref, keep, factor_ref, context_ref, left, sems, small
):
    depth = 3
    starts = [sum(blocks[:b]) for b in range(len(blocks))]
    copies = []
    for b, height in enumerate(blocks):
        rows = pl.ds(starts[b], height)
        copies.append(pltpu.make_async_copy(tensor_ref.at[rows, :], keep.at[rows, :], sems.at[b]))
    first = pltpu.make_async_copy(factor_hbm, factor_ref, small.at[0])
    second = pltpu.make_async_copy(context_hbm, context_ref, small.at[1])
    first.start()
    second.start()
    for copy in copies[:depth]:
        copy.start()
    contexts, rank = context_ref.shape
    chunks, tall, _ = out_ref.shape
    part = rank // chunks
    genes = tall - 2 * part
    first.wait()
    second.wait()
    context32 = context_ref[...].astype(f32)

    def build(b):
        perts = blocks[b] // contexts
        factor = factor_ref[pl.ds(starts[b] // contexts, perts), :].astype(f32)
        rows = (factor[:, None, :] * context32[None]).reshape(blocks[b], rank)
        hi, lo = split(rows.T)
        left[b % 2, :rank, : blocks[b]] = hi
        left[b % 2, rank:, : blocks[b]] = lo

    build(0)
    for shift, gram in enumerate(split(gram_of(factor_ref[...]))):
        for q in range(chunks):
            rows = pl.ds(genes + shift * part, part)
            out_ref[q, rows, :] = gram[q * part : (q + 1) * part, :]
    total = None
    for b in range(len(blocks)):
        copies[b].wait()
        if b + depth < len(blocks):
            copies[b + depth].start()
        if b + 1 < len(blocks):
            build(b + 1)
        product = dot(left[b % 2, :, : blocks[b]], keep[pl.ds(starts[b], blocks[b]), :])
        total = product if total is None else total + product
    summed = (total[:rank, :] + total[rank:, :]).T.astype(bf16)
    for q in range(chunks):
        out_ref[q, :genes, :] = summed[q * genes : (q + 1) * genes, :]


def narrow_sum_and_copy(part, in_ref, out_ref):
    total = jnp.sum(in_ref[...].astype(f32), axis=0)
    genes = total.shape[0] - 2 * part
    hi, lo = split(total[genes : genes + part, :] + total[genes + part :, :])
    total = jnp.concatenate([total[:genes, :].astype(bf16), hi, lo], axis=0)
    for q in range(out_ref.shape[0]):
        out_ref[q] = total


def core_sum(share, a_ref, b_ref, out_ref):
    total = a_ref[...] + b_ref[...]
    perts = total.shape[1] - share
    high, low = split(total[:, perts:, :])
    out_ref[:, :perts, :] = total[:, :perts, :].astype(bf16)
    out_ref[:, perts : perts + share, :] = high
    out_ref[:, perts + share :, :] = low


def gene_sum(share, in_ref, out_ref):
    total = jnp.sum(in_ref[...].astype(f32), axis=0)
    perts = total.shape[0] - 2 * share
    gram = total[perts : perts + share, :] + total[perts + share :, :]
    total = jnp.concatenate([total[:perts, :], gram], axis=0)
    for q in range(out_ref.shape[0]):
        out_ref[q] = total


def half_index():
    return lax.rem(lax.axis_index("gene"), 2)


def contract(blocks, core, tensor_ref, weights, context, gram_ref, out_ref):
    rank = gram_ref.shape[0]
    contexts = context.shape[0]
    context32 = context.astype(f32)
    half = tensor_ref.shape[0] // 2
    height = half // blocks
    per_block = height // contexts
    targets = out_ref.shape[0]
    perts = half // contexts // targets
    out_ref[:, perts:, :] = gram_ref[...].reshape(targets, rank // targets, rank)
    for b in range(blocks):
        start = pl.multiple_of(core * half + b * height, height)
        product = dot(tensor_ref[pl.ds(start, height), :], weights)
        wide = (product[:, :rank] + product[:, rank:]).reshape(per_block, contexts, rank)
        total = jnp.sum(wide * context32[None], axis=1)
        n = per_block // perts
        out_ref[pl.ds(b * n, n), :perts, :] = total.reshape(n, perts, rank)


def gene_solve(blocks, held_ref, context_ref, tensor_ref, other_ref, solved_ref, weights_ref, gram_ref):
    chunks, tall, rank = held_ref.shape
    part = rank // chunks
    genes = tall - 2 * part
    context = context_ref[...]
    held = held_ref[...].astype(f32)
    gram_a = (held[:, genes : genes + part, :] + held[:, genes + part :, :]).reshape(rank, rank)
    mttkrp = held[:, :genes, :].reshape(chunks * genes, rank)
    inv = inverse(gram_a * gram_of(context))
    solved = dot(mttkrp, inv, precision=HIGHEST)
    solved_ref[...] = solved
    weights = jnp.concatenate(split(solved), axis=1)
    weights_ref[...] = weights
    product = dot(weights, weights, ((0,), (0,)))
    product = product[:, :rank] + product[:, rank:]
    gram_ref[...] = product[:rank, :] + product[rank:, :]
    contract(blocks, 1 - half_index(), tensor_ref, weights, context, gram_ref, other_ref)


def pert_products(blocks, weights_ref, context_ref, tensor_ref, gram_ref, mine_ref):
    contract(
        blocks, half_index(), tensor_ref, weights_ref[...], context_ref[...], gram_ref, mine_ref
    )


def pert_inverse(gene_count, mine_ref, context_ref, inv_ref, rate_ref):
    chunks, tall, rank = mine_ref.shape
    perts = tall - rank // chunks
    gram_s = mine_ref[:, perts:, :].reshape(rank, rank)
    diag_row, _ = diagonal(gram_s, eye(rank))
    scale_c = jnp.sqrt(diag_row / gene_count + epsilon)
    rate_ref[...] = 1.0 / scale_c
    inv_ref[...] = inverse(gram_s * gram_of(context_ref[...])) * scale_c


def pert_solve(mine_ref, other_ref, inv_ref, out_ref, squares_ref):
    chunks, tall, rank = mine_ref.shape
    perts = tall - rank // chunks
    inv = inv_ref[...]
    mine = half_index()
    half = out_ref.shape[0] // 2
    squares = []
    for core, held_ref in ((mine, mine_ref), (1 - mine, other_ref)):
        mttkrp = held_ref[:, :perts, :].reshape(half, rank)
        solved = dot(mttkrp, inv, precision=HIGHEST)
        out_ref[pl.ds(pl.multiple_of(core * half, half), half), :] = solved
        squares.append(jnp.sum(solved * solved, axis=0, keepdims=True))
    squares_ref[...] = jnp.broadcast_to((squares[0] + squares[1])[None], squares_ref.shape)


def scale(pert_count, held_ref, solved_a_ref, solved_c_ref, rate_ref, gene_ref, pert_ref, gene, pert, sems):
    gene[...] = (solved_c_ref[...] * rate_ref[...]).astype(bf16)
    first = pltpu.make_async_copy(gene, gene_ref, sems.at[0])
    first.start()
    squares = jnp.sum(held_ref[...], axis=0)
    rate = 1.0 / jnp.sqrt(squares / pert_count + epsilon)
    half = pert.shape[0] // 2
    copies = []
    for h in range(2):
        rows = pl.ds(h * half, half)
        pert[rows, :] = (solved_a_ref[rows, :] * rate).astype(bf16)
        copy = pltpu.make_async_copy(pert.at[rows, :], pert_ref.at[rows, :], sems.at[1 + h])
        copy.start()
        copies.append(copy)
    first.wait()
    for copy in copies:
        copy.wait()


VMEM = pl.BlockSpec(memory_space=pltpu.VMEM)
FAR = pl.BlockSpec(memory_space=pltpu.HBM)


def near(x):
    return pltpu.with_memory_space_constraint(x, pltpu.VMEM)


def far(x):
    return pltpu.with_memory_space_constraint(x, pltpu.HBM)


def call(body, name, inputs, outputs, in_specs=None, out_spec=VMEM, scratch=(), limit=16):
    single = not isinstance(outputs, tuple)
    return pl.pallas_call(
        body,
        in_specs=in_specs or [VMEM] * len(inputs),
        out_specs=out_spec if single else (out_spec,) * len(outputs),
        out_shape=outputs,
        scratch_shapes=list(scratch),
        compiler_params=pltpu.CompilerParams(vmem_limit_bytes=limit << 20),
        name=name,
    )(*inputs)


def shards(tensor, pert_factor, context_factor):
    rows_i, contexts, rows_j = tensor.shape
    rank = pert_factor.shape[1]
    n_pert = lax.axis_size("pert")
    n_gene = lax.axis_size("gene")
    flat = tensor.reshape(rows_i * contexts, rows_j)
    eighth = rows_i * contexts // 8
    blocks = (eighth, eighth, 2 * eighth, 2 * eighth, 2 * eighth)
    part = rank // n_pert
    tall = rows_j // n_pert + 2 * part

    partial, kept = call(
        functools.partial(gene_products, blocks),
        "gene_products",
        (far(flat), far(pert_factor), far(context_factor)),
        (pltpu.VMEM((n_pert, tall, rank), bf16), pltpu.VMEM(flat.shape, bf16)),
        in_specs=[FAR] * 3,
        scratch=(
            pltpu.VMEM(pert_factor.shape, bf16),
            pltpu.VMEM(context_factor.shape, bf16),
            pltpu.VMEM((2, 2 * rank, max(blocks)), bf16),
            pltpu.SemaphoreType.DMA((len(blocks),)),
            pltpu.SemaphoreType.DMA((2,)),
        ),
    )
    partial = lax.all_to_all(partial, "pert", 0, 0)
    gathered = call(
        functools.partial(narrow_sum_and_copy, part),
        "pert_sum",
        (near(partial),),
        pltpu.VMEM(partial.shape, bf16),
    )
    gathered = lax.all_to_all(gathered, "pert", 0, 0)

    context_factor = near(context_factor)
    chips = n_gene // 2
    perts = rows_i // n_gene
    message = pltpu.VMEM((chips, perts + rank // chips, rank), f32)
    square = pltpu.VMEM((rank, rank), f32)
    kept = near(kept)
    other, solved_c, weights, gram_s = call(
        functools.partial(gene_solve, 4),
        "gene_solve",
        (near(gathered), context_factor, kept),
        (
            message,
            pltpu.VMEM((rows_j, rank), f32),
            pltpu.VMEM((rows_j, 2 * rank), bf16),
            square,
        ),
    )
    swap = [(i, i ^ 1) for i in range(n_gene)]
    groups = [[2 * i + core for i in range(chips)] for core in range(2)]
    other = lax.ppermute(other, "gene", swap)
    mine = call(
        functools.partial(pert_products, 4),
        "pert_products",
        (near(weights), context_factor, kept, near(gram_s)),
        message,
    )
    share = rank // chips
    partial = call(
        functools.partial(core_sum, share),
        "core_sum",
        (near(mine), near(other)),
        pltpu.VMEM((chips, perts + 2 * share, rank), bf16),
    )
    partial = lax.all_to_all(partial, "gene", 0, 0, axis_index_groups=groups)
    summed = call(functools.partial(gene_sum, share), "gene_sum", (near(partial),), message)
    mine = lax.all_to_all(summed, "gene", 0, 0, axis_index_groups=groups)
    other = lax.ppermute(mine, "gene", swap)
    mine = near(mine)
    inv, rate = call(
        functools.partial(pert_inverse, rows_j * n_gene),
        "pert_inverse",
        (mine, context_factor),
        (square, pltpu.VMEM((1, rank), f32)),
    )
    solved_a, squares = call(
        pert_solve,
        "pert_solve",
        (mine, near(other), near(inv)),
        (pltpu.VMEM((rows_i, rank), f32), pltpu.VMEM((n_pert, 1, rank), f32)),
    )
    squares = lax.all_to_all(squares, "pert", 0, 0)
    outputs = (
        jax.ShapeDtypeStruct((rows_j, rank), bf16),
        jax.ShapeDtypeStruct((rows_i, rank), bf16),
    )
    return call(
        functools.partial(scale, rows_i * n_pert),
        "scale",
        (near(squares), near(solved_a), near(solved_c), near(rate)),
        outputs,
        out_spec=FAR,
        scratch=[pltpu.VMEM(o.shape, bf16) for o in outputs] + [pltpu.SemaphoreType.DMA((3,))],
    )


def solution(mesh):
    return jax.shard_map(
        shards,
        mesh=mesh,
        in_specs=(P("pert", None, "gene"), P("pert", None), P()),
        out_specs=(P("gene", None), P("pert", None)),
        check_vma=False,
    )
```

```python
import functools

import jax
import jax.numpy as jnp
from jax import lax
from jax.experimental import pallas as pl
from jax.experimental.pallas import tpu as pltpu
from jax.sharding import PartitionSpec as P

epsilon = 1e-06
f32 = jnp.float32
bf16 = jnp.bfloat16
HIGHEST = lax.Precision.HIGHEST


def dot(a, b, dims=((1,), (0,)), precision=None):
    return lax.dot_general(a, b, (dims, ((), ())), precision=precision, preferred_element_type=f32)


def split(x):
    hi = x.astype(bf16)
    return hi, (x - hi.astype(f32)).astype(bf16)


def dot_split(a, b):
    n = b.shape[1]
    right = jnp.concatenate(split(b), axis=1)
    product = dot(jnp.concatenate(split(a), axis=1), jnp.concatenate([right, right], axis=0))
    return product[:, :n] + product[:, n:]


def eye(n):
    return (
        lax.broadcasted_iota(jnp.int32, (n, n), 0) == lax.broadcasted_iota(jnp.int32, (n, n), 1)
    ).astype(f32)


def diagonal(a, unit):
    picked = a * unit
    return jnp.sum(picked, axis=0, keepdims=True), jnp.sum(picked, axis=1, keepdims=True)


def row_norm(a):
    return jnp.max(jnp.sum(jnp.abs(a), axis=1, keepdims=True))


def inverse(a):
    unit = eye(a.shape[0])
    diag_row, diag_col = diagonal(a, unit)
    scale_row, scale_col = lax.rsqrt(diag_row), lax.rsqrt(diag_col)
    scaled = a * scale_col * scale_row
    off = row_norm(unit - scaled)
    far_off = off >= 0.95
    alpha = jnp.where(far_off, 1.0 / (1.0 + off), 1.0)
    r = unit - alpha * scaled
    x = alpha * (unit + r)
    r = dot_split(r, r)
    n = a.shape[0]

    def advance(x, r):
        product = dot_split(jnp.concatenate([x, r], axis=0), r)
        return x + product[:n, :], product[n:, :]

    def more(state):
        x, r, bound, count = state
        norm = row_norm(r)
        return *advance(x, r), norm * norm, count + 1

    def newton(_, x):
        return x + dot_split(x, unit - dot(scaled, x, precision=HIGHEST))

    x, r, bound, _ = lax.while_loop(
        lambda s: jnp.logical_and(s[2] > 1e-7, s[3] < 40),
        more,
        (x, r, jnp.where(far_off, 1.0, off * off), 0),
    )
    x = lax.fori_loop(0, jnp.where(far_off, 4, jnp.where(off > 0.8, 1, 0)), newton, x)
    return x * scale_col * scale_row


def gram_of(context):
    return dot(context, context, ((0,), (0,)))


def gene_products(
    blocks, tensor_ref, factor_hbm, context_hbm, out_ref, keep, factor_ref, context_ref, left, sems, small
):
    starts = [sum(blocks[:b]) for b in range(len(blocks))]
    copies = []
    for b, height in enumerate(blocks):
        rows = pl.ds(starts[b], height)
        copies.append(pltpu.make_async_copy(tensor_ref.at[rows, :], keep.at[rows, :], sems.at[b]))
    first = pltpu.make_async_copy(factor_hbm, factor_ref, small.at[0])
    second = pltpu.make_async_copy(context_hbm, context_ref, small.at[1])
    first.start()
    second.start()
    for copy in copies:
        copy.start(priority=1)
    contexts, rank = context_ref.shape
    chunks, tall, _ = out_ref.shape
    part = rank // chunks
    genes = tall - 2 * part
    first.wait()
    second.wait()
    context32 = context_ref[...].astype(f32)

    def build(b):
        perts = blocks[b] // contexts
        factor = factor_ref[pl.ds(starts[b] // contexts, perts), :].astype(f32)
        rows = (factor[:, None, :] * context32[None]).reshape(blocks[b], rank)
        hi, lo = split(rows.T)
        left[b % 2, :rank, : blocks[b]] = hi
        left[b % 2, rank:, : blocks[b]] = lo

    build(0)
    for shift, gram in enumerate(split(gram_of(factor_ref[...]))):
        for q in range(chunks):
            rows = pl.ds(genes + shift * part, part)
            out_ref[q, rows, :] = gram[q * part : (q + 1) * part, :]
    total = None
    for b in range(len(blocks)):
        copies[b].wait()
        if b + 1 < len(blocks):
            build(b + 1)
        product = dot(left[b % 2, :, : blocks[b]], keep[pl.ds(starts[b], blocks[b]), :])
        total = product if total is None else total + product
    summed = (total[:rank, :] + total[rank:, :]).T.astype(bf16)
    for q in range(chunks):
        out_ref[q, :genes, :] = summed[q * genes : (q + 1) * genes, :]


def narrow_sum_and_copy(part, in_ref, out_ref):
    total = jnp.sum(in_ref[...].astype(f32), axis=0)
    genes = total.shape[0] - 2 * part
    hi, lo = split(total[genes : genes + part, :] + total[genes + part :, :])
    total = jnp.concatenate([total[:genes, :].astype(bf16), hi, lo], axis=0)
    for q in range(out_ref.shape[0]):
        out_ref[q] = total


def core_sum(share, a_ref, b_ref, out_ref):
    total = a_ref[...] + b_ref[...]
    perts = total.shape[1] - share
    high, low = split(total[:, perts:, :])
    out_ref[:, :perts, :] = total[:, :perts, :].astype(bf16)
    out_ref[:, perts : perts + share, :] = high
    out_ref[:, perts + share :, :] = low


def gene_sum(share, in_ref, out_ref):
    total = jnp.sum(in_ref[...].astype(f32), axis=0)
    perts = total.shape[0] - 2 * share
    gram = total[perts : perts + share, :] + total[perts + share :, :]
    total = jnp.concatenate([total[:perts, :], gram], axis=0)
    for q in range(out_ref.shape[0]):
        out_ref[q] = total


def half_index():
    return lax.rem(lax.axis_index("gene"), 2)


def contract(blocks, core, tensor_ref, weights, context, gram_ref, out_ref):
    rank = gram_ref.shape[0]
    contexts = context.shape[0]
    context32 = context.astype(f32)
    half = tensor_ref.shape[0] // 2
    height = half // blocks
    per_block = height // contexts
    targets = out_ref.shape[0]
    perts = half // contexts // targets
    out_ref[:, perts:, :] = gram_ref[...].reshape(targets, rank // targets, rank)
    for b in range(blocks):
        start = pl.multiple_of(core * half + b * height, height)
        product = dot(tensor_ref[pl.ds(start, height), :], weights)
        wide = (product[:, :rank] + product[:, rank:]).reshape(per_block, contexts, rank)
        total = jnp.sum(wide * context32[None], axis=1)
        n = per_block // perts
        out_ref[pl.ds(b * n, n), :perts, :] = total.reshape(n, perts, rank)


def gene_solve(blocks, held_ref, context_ref, tensor_ref, other_ref, solved_ref, weights_ref, gram_ref):
    chunks, tall, rank = held_ref.shape
    part = rank // chunks
    genes = tall - 2 * part
    context = context_ref[...]
    rows = held_ref[:, genes:, :].astype(f32)
    gram_a = (rows[:, :part, :] + rows[:, part:, :]).reshape(rank, rank)
    mttkrp = held_ref[:, :genes, :].reshape(chunks * genes, rank)
    inv = inverse(gram_a * gram_of(context))
    high = inv.astype(bf16)
    middle, low = split(inv - high.astype(f32))
    product = dot(mttkrp, jnp.concatenate([high, middle], axis=1))
    solved = product[:, :rank] + (product[:, rank:] + dot(mttkrp, low))
    solved_ref[...] = solved
    weights = jnp.concatenate(split(solved), axis=1)
    weights_ref[...] = weights
    product = dot(weights, weights, ((0,), (0,)))
    product = product[:, :rank] + product[:, rank:]
    gram_ref[...] = product[:rank, :] + product[rank:, :]
    contract(blocks, 1 - half_index(), tensor_ref, weights, context, gram_ref, other_ref)


def pert_products(blocks, weights_ref, context_ref, tensor_ref, gram_ref, mine_ref):
    contract(
        blocks, half_index(), tensor_ref, weights_ref[...], context_ref[...], gram_ref, mine_ref
    )


def pert_inverse(gene_count, mine_ref, context_ref, inv_ref, rate_ref):
    chunks, tall, rank = mine_ref.shape
    perts = tall - rank // chunks
    gram_s = mine_ref[:, perts:, :].reshape(rank, rank)
    diag_row, _ = diagonal(gram_s, eye(rank))
    scale_c = jnp.sqrt(diag_row / gene_count + epsilon)
    rate_ref[...] = 1.0 / scale_c
    inv_ref[...] = inverse(gram_s * gram_of(context_ref[...])) * scale_c


def pert_solve(mine_ref, other_ref, inv_ref, out_ref, squares_ref):
    chunks, tall, rank = mine_ref.shape
    perts = tall - rank // chunks
    inv = inv_ref[...]
    mine = half_index()
    half = out_ref.shape[0] // 2
    squares = []
    for core, held_ref in ((mine, mine_ref), (1 - mine, other_ref)):
        mttkrp = held_ref[:, :perts, :].reshape(half, rank)
        solved = dot(mttkrp, inv, precision=HIGHEST)
        out_ref[pl.ds(pl.multiple_of(core * half, half), half), :] = solved
        squares.append(jnp.sum(solved * solved, axis=0, keepdims=True))
    squares_ref[...] = jnp.broadcast_to((squares[0] + squares[1])[None], squares_ref.shape)


def scale(pert_count, held_ref, solved_a_ref, solved_c_ref, rate_ref, gene_ref, pert_ref, gene, pert, sems):
    gene[...] = (solved_c_ref[...] * rate_ref[...]).astype(bf16)
    first = pltpu.make_async_copy(gene, gene_ref, sems.at[0])
    first.start()
    squares = jnp.sum(held_ref[...], axis=0)
    rate = 1.0 / jnp.sqrt(squares / pert_count + epsilon)
    half = pert.shape[0] // 2
    copies = []
    for h in range(2):
        rows = pl.ds(h * half, half)
        pert[rows, :] = (solved_a_ref[rows, :] * rate).astype(bf16)
        copy = pltpu.make_async_copy(pert.at[rows, :], pert_ref.at[rows, :], sems.at[1 + h])
        copy.start()
        copies.append(copy)
    first.wait()
    for copy in copies:
        copy.wait()


VMEM = pl.BlockSpec(memory_space=pltpu.VMEM)
FAR = pl.BlockSpec(memory_space=pltpu.HBM)


def near(x):
    return pltpu.with_memory_space_constraint(x, pltpu.VMEM)


def far(x):
    return pltpu.with_memory_space_constraint(x, pltpu.HBM)


def call(body, name, inputs, outputs, in_specs=None, out_spec=VMEM, scratch=(), limit=16):
    single = not isinstance(outputs, tuple)
    return pl.pallas_call(
        body,
        in_specs=in_specs or [VMEM] * len(inputs),
        out_specs=out_spec if single else (out_spec,) * len(outputs),
        out_shape=outputs,
        scratch_shapes=list(scratch),
        compiler_params=pltpu.CompilerParams(vmem_limit_bytes=limit << 20),
        name=name,
    )(*inputs)


def shards(tensor, pert_factor, context_factor):
    rows_i, contexts, rows_j = tensor.shape
    rank = pert_factor.shape[1]
    n_pert = lax.axis_size("pert")
    n_gene = lax.axis_size("gene")
    flat = tensor.reshape(rows_i * contexts, rows_j)
    eighth = rows_i * contexts // 8
    blocks = (eighth, eighth, 2 * eighth, 2 * eighth, 2 * eighth)
    part = rank // n_pert
    tall = rows_j // n_pert + 2 * part

    partial, kept = call(
        functools.partial(gene_products, blocks),
        "gene_products",
        (far(flat), far(pert_factor), far(context_factor)),
        (pltpu.VMEM((n_pert, tall, rank), bf16), pltpu.VMEM(flat.shape, bf16)),
        in_specs=[FAR] * 3,
        scratch=(
            pltpu.VMEM(pert_factor.shape, bf16),
            pltpu.VMEM(context_factor.shape, bf16),
            pltpu.VMEM((2, 2 * rank, max(blocks)), bf16),
            pltpu.SemaphoreType.DMA((len(blocks),)),
            pltpu.SemaphoreType.DMA((2,)),
        ),
    )
    partial = lax.all_to_all(partial, "pert", 0, 0)
    gathered = call(
        functools.partial(narrow_sum_and_copy, part),
        "pert_sum",
        (near(partial),),
        pltpu.VMEM(partial.shape, bf16),
    )
    gathered = lax.all_to_all(gathered, "pert", 0, 0)

    context_factor = near(context_factor)
    chips = n_gene // 2
    perts = rows_i // n_gene
    message = pltpu.VMEM((chips, perts + rank // chips, rank), f32)
    square = pltpu.VMEM((rank, rank), f32)
    kept = near(kept)
    other, solved_c, weights, gram_s = call(
        functools.partial(gene_solve, 4),
        "gene_solve",
        (near(gathered), context_factor, kept),
        (
            message,
            pltpu.VMEM((rows_j, rank), f32),
            pltpu.VMEM((rows_j, 2 * rank), bf16),
            square,
        ),
    )
    swap = [(i, i ^ 1) for i in range(n_gene)]
    groups = [[2 * i + core for i in range(chips)] for core in range(2)]
    other = lax.ppermute(other, "gene", swap)
    mine = call(
        functools.partial(pert_products, 4),
        "pert_products",
        (near(weights), context_factor, kept, near(gram_s)),
        message,
    )
    share = rank // chips
    partial = call(
        functools.partial(core_sum, share),
        "core_sum",
        (near(mine), near(other)),
        pltpu.VMEM((chips, perts + 2 * share, rank), bf16),
    )
    partial = lax.all_to_all(partial, "gene", 0, 0, axis_index_groups=groups)
    summed = call(functools.partial(gene_sum, share), "gene_sum", (near(partial),), message)
    mine = lax.all_to_all(summed, "gene", 0, 0, axis_index_groups=groups)
    other = lax.ppermute(mine, "gene", swap)
    mine = near(mine)
    inv, rate = call(
        functools.partial(pert_inverse, rows_j * n_gene),
        "pert_inverse",
        (mine, context_factor),
        (square, pltpu.VMEM((1, rank), f32)),
    )
    solved_a, squares = call(
        pert_solve,
        "pert_solve",
        (mine, near(other), near(inv)),
        (pltpu.VMEM((rows_i, rank), f32), pltpu.VMEM((n_pert, 1, rank), f32)),
    )
    squares = lax.all_to_all(squares, "pert", 0, 0)
    outputs = (
        jax.ShapeDtypeStruct((rows_j, rank), bf16),
        jax.ShapeDtypeStruct((rows_i, rank), bf16),
    )
    return call(
        functools.partial(scale, rows_i * n_pert),
        "scale",
        (near(squares), near(solved_a), near(solved_c), near(rate)),
        outputs,
        out_spec=FAR,
        scratch=[pltpu.VMEM(o.shape, bf16) for o in outputs] + [pltpu.SemaphoreType.DMA((3,))],
    )


def solution(mesh):
    return jax.shard_map(
        shards,
        mesh=mesh,
        in_specs=(P("pert", None, "gene"), P("pert", None), P()),
        out_specs=(P("gene", None), P("pert", None)),
        check_vma=False,
    )
```

```python
import functools

import jax
import jax.numpy as jnp
from jax import lax
from jax.experimental import pallas as pl
from jax.experimental.pallas import tpu as pltpu
from jax.sharding import PartitionSpec as P

epsilon = 1e-06
f32 = jnp.float32
bf16 = jnp.bfloat16
HIGHEST = lax.Precision.HIGHEST


def dot(a, b, dims=((1,), (0,)), precision=None):
    return lax.dot_general(a, b, (dims, ((), ())), precision=precision, preferred_element_type=f32)


def split(x):
    hi = x.astype(bf16)
    return hi, (x - hi.astype(f32)).astype(bf16)


def dot_split(a, b):
    n = b.shape[1]
    right = jnp.concatenate(split(b), axis=1)
    product = dot(jnp.concatenate(split(a), axis=1), jnp.concatenate([right, right], axis=0))
    return product[:, :n] + product[:, n:]


def split3(x):
    first = x.astype(bf16)
    return (first, *split(x - first.astype(f32)))


def dot_split3(a, b):
    n = b.shape[1]
    a0, a1, a2 = split3(a)
    b0, b1, b2 = split3(b)
    right = jnp.concatenate([b0, b1], axis=1)
    product = dot(jnp.concatenate([a0, a1], axis=1), jnp.concatenate([right, right], axis=0))
    rest = dot(jnp.concatenate([a2, a0], axis=1), jnp.concatenate([b0, b2], axis=0))
    return product[:, :n] + (product[:, n:] + rest)


def eye(n):
    return (
        lax.broadcasted_iota(jnp.int32, (n, n), 0) == lax.broadcasted_iota(jnp.int32, (n, n), 1)
    ).astype(f32)


def diagonal(a, unit):
    picked = a * unit
    return jnp.sum(picked, axis=0, keepdims=True), jnp.sum(picked, axis=1, keepdims=True)


def row_norm(a):
    return jnp.max(jnp.sum(jnp.abs(a), axis=1, keepdims=True))


def inverse(a):
    unit = eye(a.shape[0])
    diag_row, diag_col = diagonal(a, unit)
    scale_row, scale_col = lax.rsqrt(diag_row), lax.rsqrt(diag_col)
    scaled = a * scale_col * scale_row
    off = row_norm(unit - scaled)
    far_off = off >= 0.95
    alpha = jnp.where(far_off, 1.0 / (1.0 + off), 1.0)
    r = unit - alpha * scaled
    x = alpha * (unit + r)
    r = dot_split(r, r)
    n = a.shape[0]

    def advance(x, r):
        product = dot_split(jnp.concatenate([x, r], axis=0), r)
        return x + product[:n, :], product[n:, :]

    def more(state):
        x, r, bound, count = state
        norm = row_norm(r)
        return *advance(x, r), norm * norm, count + 1

    def newton(_, x):
        return x + dot_split(x, unit - dot(scaled, x, precision=HIGHEST))

    x, r, bound, _ = lax.while_loop(
        lambda s: jnp.logical_and(s[2] > 1e-7, s[3] < 40),
        more,
        (x, r, jnp.where(far_off, 1.0, off * off), 0),
    )
    x = lax.fori_loop(0, jnp.where(far_off, 4, jnp.where(off > 0.8, 1, 0)), newton, x)
    return x * scale_col * scale_row


def gram_of(context):
    return dot(context, context, ((0,), (0,)))


def gene_products(
    blocks, tensor_ref, factor_hbm, context_hbm, out_ref, keep, factor_ref, context_ref, left, sems, small
):
    starts = [sum(blocks[:b]) for b in range(len(blocks))]
    copies = []
    for b, height in enumerate(blocks):
        rows = pl.ds(starts[b], height)
        copies.append(pltpu.make_async_copy(tensor_ref.at[rows, :], keep.at[rows, :], sems.at[b]))
    first = pltpu.make_async_copy(factor_hbm, factor_ref, small.at[0])
    second = pltpu.make_async_copy(context_hbm, context_ref, small.at[1])
    first.start()
    second.start()
    for copy in copies:
        copy.start(priority=1)
    contexts, rank = context_ref.shape
    chunks, tall, _ = out_ref.shape
    part = rank // chunks
    genes = tall - 2 * part
    first.wait()
    second.wait()
    context32 = context_ref[...].astype(f32)

    def build(b):
        perts = blocks[b] // contexts
        factor = factor_ref[pl.ds(starts[b] // contexts, perts), :].astype(f32)
        rows = (factor[:, None, :] * context32[None]).reshape(blocks[b], rank)
        hi, lo = split(rows.T)
        left[b % 2, :rank, : blocks[b]] = hi
        left[b % 2, rank:, : blocks[b]] = lo

    build(0)
    for shift, gram in enumerate(split(gram_of(factor_ref[...]))):
        for q in range(chunks):
            rows = pl.ds(genes + shift * part, part)
            out_ref[q, rows, :] = gram[q * part : (q + 1) * part, :]
    total = None
    for b in range(len(blocks)):
        copies[b].wait()
        if b + 1 < len(blocks):
            build(b + 1)
        product = dot(left[b % 2, :, : blocks[b]], keep[pl.ds(starts[b], blocks[b]), :])
        total = product if total is None else total + product
    summed = (total[:rank, :] + total[rank:, :]).T.astype(bf16)
    for q in range(chunks):
        out_ref[q, :genes, :] = summed[q * genes : (q + 1) * genes, :]


def narrow_sum_and_copy(part, in_ref, out_ref):
    total = jnp.sum(in_ref[...].astype(f32), axis=0)
    genes = total.shape[0] - 2 * part
    hi, lo = split(total[genes : genes + part, :] + total[genes + part :, :])
    total = jnp.concatenate([total[:genes, :].astype(bf16), hi, lo], axis=0)
    for q in range(out_ref.shape[0]):
        out_ref[q] = total


def core_sum(share, a_ref, b_ref, out_ref):
    total = a_ref[...] + b_ref[...]
    perts = total.shape[1] - share
    high, low = split(total[:, perts:, :])
    out_ref[:, :perts, :] = total[:, :perts, :].astype(bf16)
    out_ref[:, perts : perts + share, :] = high
    out_ref[:, perts + share :, :] = low


def gene_sum(share, in_ref, out_ref):
    total = jnp.sum(in_ref[...].astype(f32), axis=0)
    perts = total.shape[0] - 2 * share
    gram = total[perts : perts + share, :] + total[perts + share :, :]
    total = jnp.concatenate([total[:perts, :], gram], axis=0)
    for q in range(out_ref.shape[0]):
        out_ref[q] = total


def half_index():
    return lax.rem(lax.axis_index("gene"), 2)


def contract(blocks, core, tensor_ref, weights, context, gram_ref, out_ref):
    rank = gram_ref.shape[0]
    contexts = context.shape[0]
    context32 = context.astype(f32)
    half = tensor_ref.shape[0] // 2
    height = half // blocks
    per_block = height // contexts
    targets = out_ref.shape[0]
    perts = half // contexts // targets
    out_ref[:, perts:, :] = gram_ref[...].reshape(targets, rank // targets, rank)
    for b in range(blocks):
        start = pl.multiple_of(core * half + b * height, height)
        product = dot(tensor_ref[pl.ds(start, height), :], weights)
        wide = (product[:, :rank] + product[:, rank:]).reshape(per_block, contexts, rank)
        total = jnp.sum(wide * context32[None], axis=1)
        n = per_block // perts
        out_ref[pl.ds(b * n, n), :perts, :] = total.reshape(n, perts, rank)


def gene_solve(blocks, held_ref, context_ref, tensor_ref, other_ref, solved_ref, weights_ref, gram_ref):
    chunks, tall, rank = held_ref.shape
    part = rank // chunks
    genes = tall - 2 * part
    context = context_ref[...]
    rows = held_ref[:, genes:, :].astype(f32)
    gram_a = (rows[:, :part, :] + rows[:, part:, :]).reshape(rank, rank)
    mttkrp = held_ref[:, :genes, :].reshape(chunks * genes, rank)
    inv = inverse(gram_a * gram_of(context))
    high = inv.astype(bf16)
    middle, low = split(inv - high.astype(f32))
    product = dot(mttkrp, jnp.concatenate([high, middle], axis=1))
    solved = product[:, :rank] + (product[:, rank:] + dot(mttkrp, low))
    solved_ref[...] = solved
    weights = jnp.concatenate(split(solved), axis=1)
    weights_ref[...] = weights
    product = dot(weights, weights, ((0,), (0,)))
    product = product[:, :rank] + product[:, rank:]
    gram_ref[...] = product[:rank, :] + product[rank:, :]
    contract(blocks, 1 - half_index(), tensor_ref, weights, context, gram_ref, other_ref)


def pert_products(blocks, weights_ref, context_ref, tensor_ref, gram_ref, mine_ref):
    contract(
        blocks, half_index(), tensor_ref, weights_ref[...], context_ref[...], gram_ref, mine_ref
    )


def pert_inverse(gene_count, mine_ref, context_ref, inv_ref, rate_ref):
    chunks, tall, rank = mine_ref.shape
    perts = tall - rank // chunks
    gram_s = mine_ref[:, perts:, :].reshape(rank, rank)
    diag_row, _ = diagonal(gram_s, eye(rank))
    scale_c = jnp.sqrt(diag_row / gene_count + epsilon)
    rate_ref[...] = 1.0 / scale_c
    inv_ref[...] = inverse(gram_s * gram_of(context_ref[...])) * scale_c


def pert_solve(mine_ref, other_ref, inv_ref, out_ref, squares_ref):
    chunks, tall, rank = mine_ref.shape
    perts = tall - rank // chunks
    inv = inv_ref[...]
    mine = half_index()
    half = out_ref.shape[0] // 2
    squares = []
    for core, held_ref in ((mine, mine_ref), (1 - mine, other_ref)):
        mttkrp = held_ref[:, :perts, :].reshape(half, rank)
        solved = dot_split3(mttkrp, inv)
        out_ref[pl.ds(pl.multiple_of(core * half, half), half), :] = solved
        squares.append(jnp.sum(solved * solved, axis=0, keepdims=True))
    squares_ref[...] = jnp.broadcast_to((squares[0] + squares[1])[None], squares_ref.shape)


def scale(pert_count, held_ref, solved_a_ref, solved_c_ref, rate_ref, gene_ref, pert_ref, gene, pert, sems):
    gene[...] = (solved_c_ref[...] * rate_ref[...]).astype(bf16)
    first = pltpu.make_async_copy(gene, gene_ref, sems.at[0])
    first.start()
    squares = jnp.sum(held_ref[...], axis=0)
    rate = 1.0 / jnp.sqrt(squares / pert_count + epsilon)
    pert[...] = (solved_a_ref[...] * rate).astype(bf16)
    second = pltpu.make_async_copy(pert, pert_ref, sems.at[1])
    second.start()
    first.wait()
    second.wait()


VMEM = pl.BlockSpec(memory_space=pltpu.VMEM)
FAR = pl.BlockSpec(memory_space=pltpu.HBM)


def near(x):
    return pltpu.with_memory_space_constraint(x, pltpu.VMEM)


def far(x):
    return pltpu.with_memory_space_constraint(x, pltpu.HBM)


def call(body, name, inputs, outputs, in_specs=None, out_spec=VMEM, scratch=(), limit=16):
    single = not isinstance(outputs, tuple)
    return pl.pallas_call(
        body,
        in_specs=in_specs or [VMEM] * len(inputs),
        out_specs=out_spec if single else (out_spec,) * len(outputs),
        out_shape=outputs,
        scratch_shapes=list(scratch),
        compiler_params=pltpu.CompilerParams(vmem_limit_bytes=limit << 20),
        name=name,
    )(*inputs)


def shards(tensor, pert_factor, context_factor):
    rows_i, contexts, rows_j = tensor.shape
    rank = pert_factor.shape[1]
    n_pert = lax.axis_size("pert")
    n_gene = lax.axis_size("gene")
    flat = tensor.reshape(rows_i * contexts, rows_j)
    eighth = rows_i * contexts // 8
    blocks = (eighth, eighth, 2 * eighth, 2 * eighth, 2 * eighth)
    part = rank // n_pert
    tall = rows_j // n_pert + 2 * part

    partial, kept = call(
        functools.partial(gene_products, blocks),
        "gene_products",
        (far(flat), far(pert_factor), far(context_factor)),
        (pltpu.VMEM((n_pert, tall, rank), bf16), pltpu.VMEM(flat.shape, bf16)),
        in_specs=[FAR] * 3,
        scratch=(
            pltpu.VMEM(pert_factor.shape, bf16),
            pltpu.VMEM(context_factor.shape, bf16),
            pltpu.VMEM((2, 2 * rank, max(blocks)), bf16),
            pltpu.SemaphoreType.DMA((len(blocks),)),
            pltpu.SemaphoreType.DMA((2,)),
        ),
    )
    partial = lax.all_to_all(partial, "pert", 0, 0)
    gathered = call(
        functools.partial(narrow_sum_and_copy, part),
        "pert_sum",
        (near(partial),),
        pltpu.VMEM(partial.shape, bf16),
    )
    gathered = lax.all_to_all(gathered, "pert", 0, 0)

    context_factor = near(context_factor)
    chips = n_gene // 2
    perts = rows_i // n_gene
    message = pltpu.VMEM((chips, perts + rank // chips, rank), f32)
    square = pltpu.VMEM((rank, rank), f32)
    kept = near(kept)
    other, solved_c, weights, gram_s = call(
        functools.partial(gene_solve, 4),
        "gene_solve",
        (near(gathered), context_factor, kept),
        (
            message,
            pltpu.VMEM((rows_j, rank), f32),
            pltpu.VMEM((rows_j, 2 * rank), bf16),
            square,
        ),
    )
    swap = [(i, i ^ 1) for i in range(n_gene)]
    groups = [[2 * i + core for i in range(chips)] for core in range(2)]
    other = lax.ppermute(other, "gene", swap)
    mine = call(
        functools.partial(pert_products, 4),
        "pert_products",
        (near(weights), context_factor, kept, near(gram_s)),
        message,
    )
    share = rank // chips
    partial = call(
        functools.partial(core_sum, share),
        "core_sum",
        (near(mine), near(other)),
        pltpu.VMEM((chips, perts + 2 * share, rank), bf16),
    )
    partial = lax.all_to_all(partial, "gene", 0, 0, axis_index_groups=groups)
    summed = call(functools.partial(gene_sum, share), "gene_sum", (near(partial),), message)
    mine = lax.all_to_all(summed, "gene", 0, 0, axis_index_groups=groups)
    other = lax.ppermute(mine, "gene", swap)
    mine = near(mine)
    inv, rate = call(
        functools.partial(pert_inverse, rows_j * n_gene),
        "pert_inverse",
        (mine, context_factor),
        (square, pltpu.VMEM((1, rank), f32)),
    )
    solved_a, squares = call(
        pert_solve,
        "pert_solve",
        (mine, near(other), near(inv)),
        (pltpu.VMEM((rows_i, rank), f32), pltpu.VMEM((n_pert, 1, rank), f32)),
    )
    squares = lax.all_to_all(squares, "pert", 0, 0)
    outputs = (
        jax.ShapeDtypeStruct((rows_j, rank), bf16),
        jax.ShapeDtypeStruct((rows_i, rank), bf16),
    )
    return call(
        functools.partial(scale, rows_i * n_pert),
        "scale",
        (near(squares), near(solved_a), near(solved_c), near(rate)),
        outputs,
        out_spec=FAR,
        scratch=[pltpu.VMEM(o.shape, bf16) for o in outputs] + [pltpu.SemaphoreType.DMA((2,))],
    )


def solution(mesh):
    return jax.shard_map(
        shards,
        mesh=mesh,
        in_specs=(P("pert", None, "gene"), P("pert", None), P()),
        out_specs=(P("gene", None), P("pert", None)),
        check_vma=False,
    )
```

```python
import functools

import jax
import jax.numpy as jnp
from jax import lax
from jax.experimental import pallas as pl
from jax.experimental.pallas import tpu as pltpu
from jax.sharding import PartitionSpec as P

epsilon = 1e-06
f32 = jnp.float32
bf16 = jnp.bfloat16
HIGHEST = lax.Precision.HIGHEST


def dot(a, b, dims=((1,), (0,)), precision=None):
    return lax.dot_general(a, b, (dims, ((), ())), precision=precision, preferred_element_type=f32)


def split(x):
    hi = x.astype(bf16)
    return hi, (x - hi.astype(f32)).astype(bf16)


def dot_split(a, b):
    n = b.shape[1]
    right = jnp.concatenate(split(b), axis=1)
    product = dot(jnp.concatenate(split(a), axis=1), jnp.concatenate([right, right], axis=0))
    return product[:, :n] + product[:, n:]


def split3(x):
    first = x.astype(bf16)
    return (first, *split(x - first.astype(f32)))


def dot_split3(a, b):
    n = b.shape[1]
    a0, a1, a2 = split3(a)
    b0, b1, b2 = split3(b)
    right = jnp.concatenate([b0, b1], axis=1)
    product = dot(jnp.concatenate([a0, a1], axis=1), jnp.concatenate([right, right], axis=0))
    rest = dot(jnp.concatenate([a2, a0], axis=1), jnp.concatenate([b0, b2], axis=0))
    return product[:, :n] + (product[:, n:] + rest)


def eye(n):
    return (
        lax.broadcasted_iota(jnp.int32, (n, n), 0) == lax.broadcasted_iota(jnp.int32, (n, n), 1)
    ).astype(f32)


def diagonal(a, unit):
    picked = a * unit
    return jnp.sum(picked, axis=0, keepdims=True), jnp.sum(picked, axis=1, keepdims=True)


def row_norm(a):
    return jnp.max(jnp.sum(jnp.abs(a), axis=1, keepdims=True))


def inverse(a):
    unit = eye(a.shape[0])
    diag_row, diag_col = diagonal(a, unit)
    scale_row, scale_col = lax.rsqrt(diag_row), lax.rsqrt(diag_col)
    scaled = a * scale_col * scale_row
    off = row_norm(unit - scaled)
    far_off = off >= 0.95
    alpha = jnp.where(far_off, 1.0 / (1.0 + off), 1.0)
    r = unit - alpha * scaled
    x = alpha * (unit + r)
    r = dot_split(r, r)
    n = a.shape[0]

    def advance(x, r):
        product = dot_split(jnp.concatenate([x, r], axis=0), r)
        return x + product[:n, :], product[n:, :]

    def more(state):
        x, r, bound, count = state
        norm = row_norm(r)
        return *advance(x, r), norm * norm, count + 1

    def newton(_, x):
        return x + dot_split(x, unit - dot(scaled, x, precision=HIGHEST))

    x, r = advance(x, r)
    norm = row_norm(r)
    x, r = advance(x, r)
    x, r, bound, _ = lax.while_loop(
        lambda s: jnp.logical_and(s[2] > 1e-7, s[3] < 40), more, (x, r, norm * norm, 2)
    )
    x = lax.fori_loop(0, jnp.where(far_off, 4, jnp.where(off > 0.8, 1, 0)), newton, x)
    return x * scale_col * scale_row


def gram_of(context):
    return dot(context, context, ((0,), (0,)))


def gene_products(
    blocks, tensor_ref, factor_hbm, context_hbm, out_ref, keep, factor_ref, context_ref, left, sems, small
):
    starts = [sum(blocks[:b]) for b in range(len(blocks))]
    copies = []
    for b, height in enumerate(blocks):
        rows = pl.ds(starts[b], height)
        copies.append(pltpu.make_async_copy(tensor_ref.at[rows, :], keep.at[rows, :], sems.at[b]))
    first = pltpu.make_async_copy(factor_hbm, factor_ref, small.at[0])
    second = pltpu.make_async_copy(context_hbm, context_ref, small.at[1])
    first.start()
    second.start()
    for copy in copies:
        copy.start(priority=1)
    contexts, rank = context_ref.shape
    chunks, tall, _ = out_ref.shape
    part = rank // chunks
    genes = tall - 2 * part
    first.wait()
    second.wait()
    context32 = context_ref[...].astype(f32)

    def build(b):
        perts = blocks[b] // contexts
        factor = factor_ref[pl.ds(starts[b] // contexts, perts), :].astype(f32)
        rows = (factor[:, None, :] * context32[None]).reshape(blocks[b], rank)
        hi, lo = split(rows.T)
        left[b % 2, :rank, : blocks[b]] = hi
        left[b % 2, rank:, : blocks[b]] = lo

    build(0)
    for shift, gram in enumerate(split(gram_of(factor_ref[...]))):
        for q in range(chunks):
            rows = pl.ds(genes + shift * part, part)
            out_ref[q, rows, :] = gram[q * part : (q + 1) * part, :]
    total = None
    for b in range(len(blocks)):
        copies[b].wait()
        if b + 1 < len(blocks):
            build(b + 1)
        product = dot(left[b % 2, :, : blocks[b]], keep[pl.ds(starts[b], blocks[b]), :])
        total = product if total is None else total + product
    summed = (total[:rank, :] + total[rank:, :]).T.astype(bf16)
    for q in range(chunks):
        out_ref[q, :genes, :] = summed[q * genes : (q + 1) * genes, :]


def narrow_sum_and_copy(part, in_ref, out_ref):
    total = jnp.sum(in_ref[...].astype(f32), axis=0)
    genes = total.shape[0] - 2 * part
    hi, lo = split(total[genes : genes + part, :] + total[genes + part :, :])
    total = jnp.concatenate([total[:genes, :].astype(bf16), hi, lo], axis=0)
    for q in range(out_ref.shape[0]):
        out_ref[q] = total


def core_sum(share, a_ref, b_ref, out_ref):
    total = a_ref[...] + b_ref[...]
    perts = total.shape[1] - share
    high, low = split(total[:, perts:, :])
    out_ref[:, :perts, :] = total[:, :perts, :].astype(bf16)
    out_ref[:, perts : perts + share, :] = high
    out_ref[:, perts + share :, :] = low


def gene_sum(share, in_ref, out_ref):
    total = jnp.sum(in_ref[...].astype(f32), axis=0)
    perts = total.shape[0] - 2 * share
    gram = total[perts : perts + share, :] + total[perts + share :, :]
    total = jnp.concatenate([total[:perts, :], gram], axis=0)
    for q in range(out_ref.shape[0]):
        out_ref[q] = total


def half_index():
    return lax.rem(lax.axis_index("gene"), 2)


def contract(blocks, core, tensor_ref, weights, context, gram_ref, out_ref):
    rank = gram_ref.shape[0]
    contexts = context.shape[0]
    context32 = context.astype(f32)
    half = tensor_ref.shape[0] // 2
    height = half // blocks
    per_block = height // contexts
    targets = out_ref.shape[0]
    perts = half // contexts // targets
    out_ref[:, perts:, :] = gram_ref[...].reshape(targets, rank // targets, rank)
    for b in range(blocks):
        start = pl.multiple_of(core * half + b * height, height)
        product = dot(tensor_ref[pl.ds(start, height), :], weights)
        wide = (product[:, :rank] + product[:, rank:]).reshape(per_block, contexts, rank)
        total = jnp.sum(wide * context32[None], axis=1)
        n = per_block // perts
        out_ref[pl.ds(b * n, n), :perts, :] = total.reshape(n, perts, rank)


def gene_solve(blocks, held_ref, context_ref, tensor_ref, other_ref, solved_ref, weights_ref, gram_ref):
    chunks, tall, rank = held_ref.shape
    part = rank // chunks
    genes = tall - 2 * part
    context = context_ref[...]
    rows = held_ref[:, genes:, :].astype(f32)
    gram_a = (rows[:, :part, :] + rows[:, part:, :]).reshape(rank, rank)
    mttkrp = held_ref[:, :genes, :].reshape(chunks * genes, rank)
    inv = inverse(gram_a * gram_of(context))
    high = inv.astype(bf16)
    middle, low = split(inv - high.astype(f32))
    product = dot(mttkrp, jnp.concatenate([high, middle], axis=1))
    solved = product[:, :rank] + (product[:, rank:] + dot(mttkrp, low))
    solved_ref[...] = solved
    weights = jnp.concatenate(split(solved), axis=1)
    weights_ref[...] = weights
    product = dot(weights, weights, ((0,), (0,)))
    product = product[:, :rank] + product[:, rank:]
    gram_ref[...] = product[:rank, :] + product[rank:, :]
    contract(blocks, 1 - half_index(), tensor_ref, weights, context, gram_ref, other_ref)


def pert_products(blocks, weights_ref, context_ref, tensor_ref, gram_ref, mine_ref):
    contract(
        blocks, half_index(), tensor_ref, weights_ref[...], context_ref[...], gram_ref, mine_ref
    )


def pert_inverse(gene_count, mine_ref, context_ref, inv_ref, rate_ref):
    chunks, tall, rank = mine_ref.shape
    perts = tall - rank // chunks
    gram_s = mine_ref[:, perts:, :].reshape(rank, rank)
    diag_row, _ = diagonal(gram_s, eye(rank))
    scale_c = jnp.sqrt(diag_row / gene_count + epsilon)
    rate_ref[...] = 1.0 / scale_c
    inv_ref[...] = inverse(gram_s * gram_of(context_ref[...])) * scale_c


def pert_solve(mine_ref, other_ref, inv_ref, out_ref, squares_ref):
    chunks, tall, rank = mine_ref.shape
    perts = tall - rank // chunks
    inv = inv_ref[...]
    mine = half_index()
    half = out_ref.shape[0] // 2
    squares = []
    for core, held_ref in ((mine, mine_ref), (1 - mine, other_ref)):
        mttkrp = held_ref[:, :perts, :].reshape(half, rank)
        solved = dot_split3(mttkrp, inv)
        out_ref[pl.ds(pl.multiple_of(core * half, half), half), :] = solved
        squares.append(jnp.sum(solved * solved, axis=0, keepdims=True))
    squares_ref[...] = jnp.broadcast_to((squares[0] + squares[1])[None], squares_ref.shape)


def scale(pert_count, held_ref, solved_a_ref, solved_c_ref, rate_ref, gene_ref, pert_ref, gene, pert, sems):
    gene[...] = (solved_c_ref[...] * rate_ref[...]).astype(bf16)
    first = pltpu.make_async_copy(gene, gene_ref, sems.at[0])
    first.start()
    squares = jnp.sum(held_ref[...], axis=0)
    rate = 1.0 / jnp.sqrt(squares / pert_count + epsilon)
    pert[...] = (solved_a_ref[...] * rate).astype(bf16)
    second = pltpu.make_async_copy(pert, pert_ref, sems.at[1])
    second.start()
    first.wait()
    second.wait()


VMEM = pl.BlockSpec(memory_space=pltpu.VMEM)
FAR = pl.BlockSpec(memory_space=pltpu.HBM)


def near(x):
    return pltpu.with_memory_space_constraint(x, pltpu.VMEM)


def far(x):
    return pltpu.with_memory_space_constraint(x, pltpu.HBM)


def call(body, name, inputs, outputs, in_specs=None, out_spec=VMEM, scratch=(), limit=16):
    single = not isinstance(outputs, tuple)
    return pl.pallas_call(
        body,
        in_specs=in_specs or [VMEM] * len(inputs),
        out_specs=out_spec if single else (out_spec,) * len(outputs),
        out_shape=outputs,
        scratch_shapes=list(scratch),
        compiler_params=pltpu.CompilerParams(vmem_limit_bytes=limit << 20),
        name=name,
    )(*inputs)


def shards(tensor, pert_factor, context_factor):
    rows_i, contexts, rows_j = tensor.shape
    rank = pert_factor.shape[1]
    n_pert = lax.axis_size("pert")
    n_gene = lax.axis_size("gene")
    flat = tensor.reshape(rows_i * contexts, rows_j)
    eighth = rows_i * contexts // 8
    blocks = (eighth, eighth, 2 * eighth, 2 * eighth, 2 * eighth)
    part = rank // n_pert
    tall = rows_j // n_pert + 2 * part

    partial, kept = call(
        functools.partial(gene_products, blocks),
        "gene_products",
        (far(flat), far(pert_factor), far(context_factor)),
        (pltpu.VMEM((n_pert, tall, rank), bf16), pltpu.VMEM(flat.shape, bf16)),
        in_specs=[FAR] * 3,
        scratch=(
            pltpu.VMEM(pert_factor.shape, bf16),
            pltpu.VMEM(context_factor.shape, bf16),
            pltpu.VMEM((2, 2 * rank, max(blocks)), bf16),
            pltpu.SemaphoreType.DMA((len(blocks),)),
            pltpu.SemaphoreType.DMA((2,)),
        ),
    )
    partial = lax.all_to_all(partial, "pert", 0, 0)
    gathered = call(
        functools.partial(narrow_sum_and_copy, part),
        "pert_sum",
        (near(partial),),
        pltpu.VMEM(partial.shape, bf16),
    )
    gathered = lax.all_to_all(gathered, "pert", 0, 0)

    context_factor = near(context_factor)
    chips = n_gene // 2
    perts = rows_i // n_gene
    message = pltpu.VMEM((chips, perts + rank // chips, rank), f32)
    square = pltpu.VMEM((rank, rank), f32)
    kept = near(kept)
    other, solved_c, weights, gram_s = call(
        functools.partial(gene_solve, 4),
        "gene_solve",
        (near(gathered), context_factor, kept),
        (
            message,
            pltpu.VMEM((rows_j, rank), f32),
            pltpu.VMEM((rows_j, 2 * rank), bf16),
            square,
        ),
    )
    swap = [(i, i ^ 1) for i in range(n_gene)]
    groups = [[2 * i + core for i in range(chips)] for core in range(2)]
    other = lax.ppermute(other, "gene", swap)
    mine = call(
        functools.partial(pert_products, 4),
        "pert_products",
        (near(weights), context_factor, kept, near(gram_s)),
        message,
    )
    share = rank // chips
    partial = call(
        functools.partial(core_sum, share),
        "core_sum",
        (near(mine), near(other)),
        pltpu.VMEM((chips, perts + 2 * share, rank), bf16),
    )
    partial = lax.all_to_all(partial, "gene", 0, 0, axis_index_groups=groups)
    summed = call(functools.partial(gene_sum, share), "gene_sum", (near(partial),), message)
    mine = lax.all_to_all(summed, "gene", 0, 0, axis_index_groups=groups)
    other = lax.ppermute(mine, "gene", swap)
    mine = near(mine)
    inv, rate = call(
        functools.partial(pert_inverse, rows_j * n_gene),
        "pert_inverse",
        (mine, context_factor),
        (square, pltpu.VMEM((1, rank), f32)),
    )
    solved_a, squares = call(
        pert_solve,
        "pert_solve",
        (mine, near(other), near(inv)),
        (pltpu.VMEM((rows_i, rank), f32), pltpu.VMEM((n_pert, 1, rank), f32)),
    )
    squares = lax.all_to_all(squares, "pert", 0, 0)
    outputs = (
        jax.ShapeDtypeStruct((rows_j, rank), bf16),
        jax.ShapeDtypeStruct((rows_i, rank), bf16),
    )
    return call(
        functools.partial(scale, rows_i * n_pert),
        "scale",
        (near(squares), near(solved_a), near(solved_c), near(rate)),
        outputs,
        out_spec=FAR,
        scratch=[pltpu.VMEM(o.shape, bf16) for o in outputs] + [pltpu.SemaphoreType.DMA((2,))],
    )


def solution(mesh):
    return jax.shard_map(
        shards,
        mesh=mesh,
        in_specs=(P("pert", None, "gene"), P("pert", None), P()),
        out_specs=(P("gene", None), P("pert", None)),
        check_vma=False,
    )
```

```python
import functools

import jax
import jax.numpy as jnp
from jax import lax
from jax.experimental import pallas as pl
from jax.experimental.pallas import tpu as pltpu
from jax.sharding import PartitionSpec as P

epsilon = 1e-06
f32 = jnp.float32
bf16 = jnp.bfloat16
HIGHEST = lax.Precision.HIGHEST


def dot(a, b, dims=((1,), (0,)), precision=None):
    return lax.dot_general(a, b, (dims, ((), ())), precision=precision, preferred_element_type=f32)


def split(x):
    hi = x.astype(bf16)
    return hi, (x - hi.astype(f32)).astype(bf16)


def dot_split(a, b):
    n = b.shape[1]
    right = jnp.concatenate(split(b), axis=1)
    product = dot(jnp.concatenate(split(a), axis=1), jnp.concatenate([right, right], axis=0))
    return product[:, :n] + product[:, n:]


def split3(x):
    first = x.astype(bf16)
    return (first, *split(x - first.astype(f32)))


def dot_split3(a, b):
    n = b.shape[1]
    a0, a1, a2 = split3(a)
    b0, b1, b2 = split3(b)
    right = jnp.concatenate([b0, b1], axis=1)
    product = dot(jnp.concatenate([a0, a1], axis=1), jnp.concatenate([right, right], axis=0))
    rest = dot(jnp.concatenate([a2, a0], axis=1), jnp.concatenate([b0, b2], axis=0))
    return product[:, :n] + (product[:, n:] + rest)


def eye(n):
    return (
        lax.broadcasted_iota(jnp.int32, (n, n), 0) == lax.broadcasted_iota(jnp.int32, (n, n), 1)
    ).astype(f32)


def diagonal(a, unit):
    picked = a * unit
    return jnp.sum(picked, axis=0, keepdims=True), jnp.sum(picked, axis=1, keepdims=True)


def row_norm(a):
    return jnp.max(jnp.sum(jnp.abs(a), axis=1, keepdims=True))


def inverse(a):
    unit = eye(a.shape[0])
    diag_row, diag_col = diagonal(a, unit)
    scale_row, scale_col = lax.rsqrt(diag_row), lax.rsqrt(diag_col)
    scaled = a * scale_col * scale_row
    off = row_norm(unit - scaled)
    far_off = off >= 0.95
    alpha = jnp.where(far_off, 1.0 / (1.0 + off), 1.0)
    r = unit - alpha * scaled
    x = alpha * (unit + r)
    r = dot_split(r, r)
    n = a.shape[0]

    def advance(x, r):
        product = dot_split(jnp.concatenate([x, r], axis=0), r)
        return x + product[:n, :], product[n:, :]

    def more(state):
        x, r, bound, count = state
        norm = row_norm(r)
        return *advance(x, r), norm * norm, count + 1

    def newton(_, x):
        return x + dot_split(x, unit - dot(scaled, x, precision=HIGHEST))

    x, r = advance(x, r)
    norm = row_norm(r)
    x, r = advance(x, r)
    x, r, bound, _ = lax.while_loop(
        lambda s: jnp.logical_and(s[2] > 1e-7, s[3] < 40), more, (x, r, norm * norm, 2)
    )
    x = lax.fori_loop(0, jnp.where(far_off, 4, jnp.where(off > 0.8, 1, 0)), newton, x)
    return x * scale_col * scale_row


def gram_of(context):
    return dot(context, context, ((0,), (0,)))


def gene_products(
    blocks, tensor_ref, factor_hbm, context_hbm, out_ref, keep, factor_ref, context_ref, left, sems, small
):
    starts = [sum(blocks[:b]) for b in range(len(blocks))]
    copies = []
    for b, height in enumerate(blocks):
        rows = pl.ds(starts[b], height)
        copies.append(pltpu.make_async_copy(tensor_ref.at[rows, :], keep.at[rows, :], sems.at[b]))
    first = pltpu.make_async_copy(factor_hbm, factor_ref, small.at[0])
    second = pltpu.make_async_copy(context_hbm, context_ref, small.at[1])
    first.start()
    second.start()
    for copy in copies:
        copy.start(priority=1)
    contexts, rank = context_ref.shape
    chunks, tall, _ = out_ref.shape
    part = rank // chunks
    genes = tall - 2 * part
    first.wait()
    second.wait()
    context32 = context_ref[...].astype(f32)

    def build(b):
        perts = blocks[b] // contexts
        factor = factor_ref[pl.ds(starts[b] // contexts, perts), :].astype(f32)
        rows = (factor[:, None, :] * context32[None]).reshape(blocks[b], rank)
        hi, lo = split(rows.T)
        left[b % 2, :rank, : blocks[b]] = hi
        left[b % 2, rank:, : blocks[b]] = lo

    build(0)
    for shift, gram in enumerate(split(gram_of(factor_ref[...]))):
        for q in range(chunks):
            rows = pl.ds(genes + shift * part, part)
            out_ref[q, rows, :] = gram[q * part : (q + 1) * part, :]
    total = None
    for b in range(len(blocks)):
        copies[b].wait()
        if b + 1 < len(blocks):
            build(b + 1)
        product = dot(left[b % 2, :, : blocks[b]], keep[pl.ds(starts[b], blocks[b]), :])
        total = product if total is None else total + product
    summed = (total[:rank, :] + total[rank:, :]).T.astype(bf16)
    for q in range(chunks):
        out_ref[q, :genes, :] = summed[q * genes : (q + 1) * genes, :]


def narrow_sum_and_copy(part, in_ref, out_ref):
    total = jnp.sum(in_ref[...].astype(f32), axis=0)
    genes = total.shape[0] - 2 * part
    hi, lo = split(total[genes : genes + part, :] + total[genes + part :, :])
    total = jnp.concatenate([total[:genes, :].astype(bf16), hi, lo], axis=0)
    for q in range(out_ref.shape[0]):
        out_ref[q] = total


def core_sum(share, a_ref, b_ref, out_ref):
    total = a_ref[...] + b_ref[...]
    perts = total.shape[1] - share
    high, low = split(total[:, perts:, :])
    out_ref[:, :perts, :] = total[:, :perts, :].astype(bf16)
    out_ref[:, perts : perts + share, :] = high
    out_ref[:, perts + share :, :] = low


def gene_sum(share, in_ref, out_ref):
    total = jnp.sum(in_ref[...].astype(f32), axis=0)
    perts = total.shape[0] - 2 * share
    gram = total[perts : perts + share, :] + total[perts + share :, :]
    total = jnp.concatenate([total[:perts, :], gram], axis=0)
    for q in range(out_ref.shape[0]):
        out_ref[q] = total


def half_index():
    return lax.rem(lax.axis_index("gene"), 2)


def contract(blocks, core, tensor_ref, weights, context, gram_ref, out_ref):
    rank = gram_ref.shape[0]
    contexts = context.shape[0]
    context32 = context.astype(f32)
    half = tensor_ref.shape[0] // 2
    height = half // blocks
    per_block = height // contexts
    targets = out_ref.shape[0]
    perts = half // contexts // targets
    out_ref[:, perts:, :] = gram_ref[...].reshape(targets, rank // targets, rank)
    for b in range(blocks):
        start = pl.multiple_of(core * half + b * height, height)
        product = dot(tensor_ref[pl.ds(start, height), :], weights)
        wide = (product[:, :rank] + product[:, rank:]).reshape(per_block, contexts, rank)
        total = jnp.sum(wide * context32[None], axis=1)
        n = per_block // perts
        out_ref[pl.ds(b * n, n), :perts, :] = total.reshape(n, perts, rank)


def gene_solve(blocks, held_ref, context_ref, tensor_ref, other_ref, solved_ref, weights_ref, gram_ref):
    chunks, tall, rank = held_ref.shape
    part = rank // chunks
    genes = tall - 2 * part
    context = context_ref[...]
    rows = held_ref[:, genes:, :].astype(f32)
    gram_a = (rows[:, :part, :] + rows[:, part:, :]).reshape(rank, rank)
    mttkrp = held_ref[:, :genes, :].reshape(chunks * genes, rank)
    inv = inverse(gram_a * gram_of(context))
    high = inv.astype(bf16)
    middle, low = split(inv - high.astype(f32))
    product = dot(mttkrp, jnp.concatenate([high, middle], axis=1))
    solved = product[:, :rank] + (product[:, rank:] + dot(mttkrp, low))
    solved_ref[...] = solved
    weights = jnp.concatenate(split(solved), axis=1)
    weights_ref[...] = weights
    product = dot(weights, weights, ((0,), (0,)))
    product = product[:, :rank] + product[:, rank:]
    gram_ref[...] = product[:rank, :] + product[rank:, :]
    contract(blocks, 1 - half_index(), tensor_ref, weights, context, gram_ref, other_ref)


def pert_products(blocks, weights_ref, context_ref, tensor_ref, gram_ref, mine_ref):
    contract(
        blocks, half_index(), tensor_ref, weights_ref[...], context_ref[...], gram_ref, mine_ref
    )


def pert_inverse(gene_count, mine_ref, context_ref, inv_ref, rate_ref):
    chunks, tall, rank = mine_ref.shape
    perts = tall - rank // chunks
    gram_s = mine_ref[:, perts:, :].reshape(rank, rank)
    diag_row, _ = diagonal(gram_s, eye(rank))
    scale_c = jnp.sqrt(diag_row / gene_count + epsilon)
    rate_ref[...] = 1.0 / scale_c
    inv_ref[...] = inverse(gram_s * gram_of(context_ref[...])) * scale_c


def pert_solve(mine_ref, other_ref, inv_ref, out_ref, squares_ref):
    chunks, tall, rank = mine_ref.shape
    perts = tall - rank // chunks
    inv = inv_ref[...]
    mine = half_index()
    half = out_ref.shape[0] // 2
    squares = []
    for core, held_ref in ((mine, mine_ref), (1 - mine, other_ref)):
        mttkrp = held_ref[:, :perts, :].reshape(half, rank)
        solved = dot_split3(mttkrp, inv)
        out_ref[pl.ds(pl.multiple_of(core * half, half), half), :] = solved
        squares.append(jnp.sum(solved * solved, axis=0, keepdims=True))
    squares_ref[...] = jnp.broadcast_to((squares[0] + squares[1])[None], squares_ref.shape)


def scale(pert_count, held_ref, solved_a_ref, solved_c_ref, rate_ref, gene_ref, pert_ref, gene, pert, sems):
    gene[...] = (solved_c_ref[...] * rate_ref[...]).astype(bf16)
    first = pltpu.make_async_copy(gene, gene_ref, sems.at[0])
    first.start()
    squares = jnp.sum(held_ref[...], axis=0)
    rate = 1.0 / jnp.sqrt(squares / pert_count + epsilon)
    pert[...] = (solved_a_ref[...] * rate).astype(bf16)
    second = pltpu.make_async_copy(pert, pert_ref, sems.at[1])
    second.start()
    first.wait()
    second.wait()


VMEM = pl.BlockSpec(memory_space=pltpu.VMEM)
FAR = pl.BlockSpec(memory_space=pltpu.HBM)


def near(x):
    return pltpu.with_memory_space_constraint(x, pltpu.VMEM)


def far(x):
    return pltpu.with_memory_space_constraint(x, pltpu.HBM)


def call(body, name, inputs, outputs, in_specs=None, out_spec=VMEM, scratch=(), limit=16):
    single = not isinstance(outputs, tuple)
    return pl.pallas_call(
        body,
        in_specs=in_specs or [VMEM] * len(inputs),
        out_specs=out_spec if single else (out_spec,) * len(outputs),
        out_shape=outputs,
        scratch_shapes=list(scratch),
        compiler_params=pltpu.CompilerParams(vmem_limit_bytes=limit << 20),
        name=name,
    )(*inputs)


def shards(tensor, pert_factor, context_factor):
    rows_i, contexts, rows_j = tensor.shape
    rank = pert_factor.shape[1]
    n_pert = lax.axis_size("pert")
    n_gene = lax.axis_size("gene")
    flat = tensor.reshape(rows_i * contexts, rows_j)
    eighth = rows_i * contexts // 8
    blocks = (eighth, eighth, 2 * eighth, 2 * eighth, 2 * eighth)
    part = rank // n_pert
    tall = rows_j // n_pert + 2 * part

    partial, kept = call(
        functools.partial(gene_products, blocks),
        "gene_products",
        (far(flat), far(pert_factor), far(context_factor)),
        (pltpu.VMEM((n_pert, tall, rank), bf16), pltpu.VMEM(flat.shape, bf16)),
        in_specs=[FAR] * 3,
        scratch=(
            pltpu.VMEM(pert_factor.shape, bf16),
            pltpu.VMEM(context_factor.shape, bf16),
            pltpu.VMEM((2, 2 * rank, max(blocks)), bf16),
            pltpu.SemaphoreType.DMA((len(blocks),)),
            pltpu.SemaphoreType.DMA((2,)),
        ),
    )
    partial = lax.all_to_all(partial, "pert", 0, 0)
    gathered = call(
        functools.partial(narrow_sum_and_copy, part),
        "pert_sum",
        (near(partial),),
        pltpu.VMEM(partial.shape, bf16),
    )
    gathered = lax.all_to_all(gathered, "pert", 0, 0)

    context_factor = near(context_factor)
    chips = n_gene // 2
    perts = rows_i // n_gene
    message = pltpu.VMEM((chips, perts + rank // chips, rank), f32)
    square = pltpu.VMEM((rank, rank), f32)
    kept = near(kept)
    other, solved_c, weights, gram_s = call(
        functools.partial(gene_solve, 2),
        "gene_solve",
        (near(gathered), context_factor, kept),
        (
            message,
            pltpu.VMEM((rows_j, rank), f32),
            pltpu.VMEM((rows_j, 2 * rank), bf16),
            square,
        ),
    )
    swap = [(i, i ^ 1) for i in range(n_gene)]
    groups = [[2 * i + core for i in range(chips)] for core in range(2)]
    other = lax.ppermute(other, "gene", swap)
    mine = call(
        functools.partial(pert_products, 2),
        "pert_products",
        (near(weights), context_factor, kept, near(gram_s)),
        message,
    )
    share = rank // chips
    partial = call(
        functools.partial(core_sum, share),
        "core_sum",
        (near(mine), near(other)),
        pltpu.VMEM((chips, perts + 2 * share, rank), bf16),
    )
    partial = lax.all_to_all(partial, "gene", 0, 0, axis_index_groups=groups)
    summed = call(functools.partial(gene_sum, share), "gene_sum", (near(partial),), message)
    mine = lax.all_to_all(summed, "gene", 0, 0, axis_index_groups=groups)
    other = lax.ppermute(mine, "gene", swap)
    mine = near(mine)
    inv, rate = call(
        functools.partial(pert_inverse, rows_j * n_gene),
        "pert_inverse",
        (mine, context_factor),
        (square, pltpu.VMEM((1, rank), f32)),
    )
    solved_a, squares = call(
        pert_solve,
        "pert_solve",
        (mine, near(other), near(inv)),
        (pltpu.VMEM((rows_i, rank), f32), pltpu.VMEM((n_pert, 1, rank), f32)),
    )
    squares = lax.all_to_all(squares, "pert", 0, 0)
    outputs = (
        jax.ShapeDtypeStruct((rows_j, rank), bf16),
        jax.ShapeDtypeStruct((rows_i, rank), bf16),
    )
    return call(
        functools.partial(scale, rows_i * n_pert),
        "scale",
        (near(squares), near(solved_a), near(solved_c), near(rate)),
        outputs,
        out_spec=FAR,
        scratch=[pltpu.VMEM(o.shape, bf16) for o in outputs] + [pltpu.SemaphoreType.DMA((2,))],
    )


def solution(mesh):
    return jax.shard_map(
        shards,
        mesh=mesh,
        in_specs=(P("pert", None, "gene"), P("pert", None), P()),
        out_specs=(P("gene", None), P("pert", None)),
        check_vma=False,
    )
```
